128 devices in a mesh: arc: 16 (over z, y_lo, core), col: 8 (over x, y_hi).
Axes of the slice: x: 4, y: 4 (y_hi: 2, y_lo: 2; y = y_hi * 2 + y_lo), z: 4, core: 2. Of those that a mesh axis runs over, the one named last changes fastest.
Arguments:
- design: bfloat16 [24576, 5120], P('arc', 'col'), may hold values from -0.109375 to 0.109375
- local_design: float32 [16, 24576], P(None, 'arc'), may hold values from -6 to 6
- observed: float32 [24576], P('arc'), may hold values from -6 to 6
- valid_mask: int32 [24576], P('arc'), may hold values 0 or 1
- counts: int32 [128], P('arc'), may hold values from 1 to 192, 15360 in all
Outputs:
- normal: float32 [5120, 5120], P('arc', 'col')
- rhs: float32 [5120], P('col')
The draws below stay inside these ranges and needn't reach their ends.
Inputs may be any that keep to these rules, and one draw needn't show every extreme that they name: Arc a holds counts[a] recorded slots at its start; the rest are padding.
All inputs are finite; a program needn't handle non-finite values. No bound on the sum of `valid_mask` or of `counts` on one device may be relied on, other than what follows from the above.
Results may differ from the reference program's by a relative error of at most 0.0028.
Values may be sent and summed in bfloat16 or wider, within the bound.
No kernel may reach another device: no remote copies, remote signals or barrier semaphores. Data moves between devices by JAX's collectives and lax.ppermute only.
A program may use at most 128 MiB of HBM per device.

```python
import math
import jax
import jax.numpy as jnp
import numpy as np
from jax import lax

COEFS = 5120
LOCAL = 16
SLOTS = 192
ARCS_DEV = 8
ARCS = 128
ROWS = 24576


def plant(array, own_key, smallest, largest):
    longest = array.shape.index(max(array.shape))
    spots = []
    for shift in (0, 1):
        where = [jax.random.randint(jax.random.fold_in(own_key, axis), (), 0, length) for axis, length in enumerate(array.shape)]
        where[longest] = (where[longest] + shift) % array.shape[longest]
        spots.append(tuple(where))
    return array.at[spots[0]].set(smallest).at[spots[1]].set(largest)


def with_spikes(array, key, source, target, parts, factor):
    owner, partner = [(jnp.arange(array.shape[dim]) // (array.shape[dim] // parts)).reshape([-1 if axis == dim else 1 for axis in range(array.ndim)]) for dim in (source, target)]
    chosen = jax.random.permutation(key, parts)[partner]
    strong = (owner == chosen) | (owner == (partner + parts // 2) % parts)
    return jnp.where(strong, factor * array, array)


def steps_of(own_key, shape, split, least, top_value):
    level, own = 1.0, jax.random.fold_in(own_key, 6)
    for dim, parts in split:
        steps = jnp.exp(jax.random.uniform(jax.random.fold_in(own, dim), (parts,), jnp.float32, least / len(split), top_value / len(split)))
        level = level * jnp.repeat(steps, shape[dim] // parts).reshape([-1 if axis == dim else 1 for axis in range(len(shape))])
    return level


def split_up(number_of, total, reach, lean):
    weights = [(1 << 20) // math.isqrt(grade ** lean) + 1 for grade in range(2, number_of + 1)]
    surplus, holding = total - reach - (number_of - 1), [1] * (number_of - 1)
    while surplus > 0:
        free = [i for i in range(number_of - 1) if holding[i] < reach]
        whole, left = sum([weights[i] for i in free]), surplus
        for i in free:
            more = min(reach - holding[i], max(1, left * weights[i] // whole), surplus)
            holding[i] = holding[i] + more
            surplus = surplus - more
    return np.array([reach] + holding)


def uneven_parts(stream_key, amount, total, limit, lean):
    if amount == 2:
        one = jax.random.randint(stream_key, (), max(1, total - limit), min(limit, total - 1) + 1)
        return jnp.stack([one, total - one])
    lengths = jnp.asarray(split_up(amount, total, limit, lean), jnp.int32)
    couples = (amount - 1) // 2
    donor, sink = lengths[1:1 + 2 * couples:2], lengths[2:2 + 2 * couples:2]
    slack = jnp.minimum(donor - 1, limit - sink)
    moved = jax.random.randint(jax.random.fold_in(stream_key, 1), (couples,), 0, 1 << 20) % (slack + 1)
    lengths = lengths.at[1:1 + 2 * couples:2].set(donor - moved).at[2:2 + 2 * couples:2].set(sink + moved)
    return lengths[jax.random.permutation(jax.random.fold_in(stream_key, 2), amount)]


def scatter_about(rng, extent, width, reach, cuts=(), kind=jnp.bfloat16):
    gain = steps_of(rng, extent, cuts, -0.22, 0.18) if cuts else 1.0
    values = jax.random.normal(rng, extent, jnp.float32) * width * gain
    return jnp.minimum(jnp.maximum(values, -reach), reach).astype(kind)


def bell_draw_with(stream_key, extent, scale, most, cuts, heavy, kind=jnp.bfloat16):
    values = scale * jax.random.normal(stream_key, extent, jnp.float32)
    if cuts:
        values = values * steps_of(stream_key, extent, cuts, -0.22, 0.18)
    return jnp.clip(with_spikes(values, jax.random.fold_in(stream_key, 3), *heavy), -most, most).astype(kind)


def setup_inputs(seed: int = 0) -> dict:
    key_of = jax.random.split(jax.random.key(seed), 6)
    design = bell_draw_with(key_of[0], (ROWS, COEFS), (ARCS_DEV * SLOTS * 4) ** -0.5, 0.109375, ((0, 16), (1, 8)), (0, 1, 16, 2.0))
    local_design = scatter_about(key_of[1], (LOCAL, ROWS), 1.0, 6.0, ((1, 16),), jnp.float32)
    observed = scatter_about(key_of[2], (ROWS,), 1.0, 6.0, ((0, 16),), jnp.float32)
    valid_mask = plant((jax.random.randint(key_of[3], (ROWS,), 0, 10) < 9).astype(jnp.int32), jax.random.fold_in(key_of[3], 1), 0, 1)
    counts = uneven_parts(key_of[4], ARCS, ARCS * SLOTS * 5 // 8, SLOTS, 2).astype(jnp.int32)
    return dict(design=design, local_design=local_design, observed=observed, valid_mask=valid_mask, counts=counts)


def eliminate(block_design, block_local, block_observed, block_live):
    highest = lax.Precision.HIGHEST
    masked = block_local * block_live[None, :]
    gram_matrix = jnp.dot(masked, block_local.T, precision=highest) + jnp.eye(block_local.shape[0], dtype=jnp.float32)
    factor = jnp.linalg.cholesky(gram_matrix)
    inverse = jax.scipy.linalg.cho_solve((factor, True), jnp.eye(block_local.shape[0], dtype=jnp.float32))
    dense = block_design.astype(jnp.float32)
    cross_terms = jnp.dot(masked, dense, precision=highest)
    cross_obs = jnp.dot(masked, block_observed, precision=highest)
    projector = jnp.dot(inverse, cross_terms, precision=highest)
    projected = block_live[:, None] * (dense - jnp.dot(block_local.T, projector, precision=highest))
    solved_obs = jnp.dot(inverse, cross_obs, precision=highest)
    residual = block_live * (block_observed - jnp.dot(block_local.T, solved_obs, precision=highest))
    return (projected.astype(jnp.bfloat16), residual)

def live_rows(counts, valid_mask):
    slot_count = valid_mask.shape[0] // counts.shape[0]
    inside = jnp.arange(slot_count, dtype=jnp.int32)[None, :] < counts[:, None]
    return inside.reshape(-1).astype(jnp.float32) * valid_mask.astype(jnp.float32)

def reference(design, local_design, observed, valid_mask, counts):
    live_mask = live_rows(counts, valid_mask)
    blocks_design = design.reshape(ARCS, SLOTS, COEFS)
    blocks_local = local_design.reshape(LOCAL, ARCS, SLOTS).transpose(1, 0, 2)
    projected, residual = jax.vmap(eliminate)(blocks_design, blocks_local, observed.reshape(ARCS, SLOTS), live_mask.reshape(ARCS, SLOTS))
    dense = projected.reshape(ROWS, COEFS).astype(jnp.float32)
    normal = jnp.dot(dense.T.astype(jnp.float32), dense.astype(jnp.float32), preferred_element_type=jnp.float32)
    rhs = jnp.dot(residual.reshape(ROWS), dense, precision=lax.Precision.HIGHEST)
    return (normal, rhs)
```

```python
import jax
import jax.numpy as jnp
from jax import lax
from jax.sharding import Mesh, PartitionSpec as P

LOCAL = 16
SLOTS = 192
AXES = ("z", "yl", "core", "x", "yh")
HIGHEST = lax.Precision.HIGHEST
F32 = jnp.float32
BF16 = jnp.bfloat16


def live_rows(counts, valid_mask):
    slot_count = valid_mask.shape[0] // counts.shape[0]
    inside = jnp.arange(slot_count, dtype=jnp.int32)[None, :] < counts[:, None]
    return inside.astype(F32) * valid_mask.reshape(inside.shape).astype(F32)


def eliminators(local, observed, live):
    arcs = live.shape[0]
    block = local.reshape(LOCAL, arcs, SLOTS).transpose(1, 0, 2)
    masked = block * live[:, None, :]
    gram = jnp.einsum("aks,als->akl", masked, block, precision=HIGHEST)
    gram = gram + jnp.eye(LOCAL, dtype=F32)
    factor = jnp.linalg.cholesky(gram)
    eye = jnp.broadcast_to(jnp.eye(LOCAL, dtype=F32), gram.shape)
    inverse = jax.vmap(lambda f, e: jax.scipy.linalg.cho_solve((f, True), e))(factor, eye)
    weights = jnp.einsum("akl,als->aks", inverse, masked, precision=HIGHEST)
    fitted = jnp.einsum("akr,aks->ars", masked, weights, precision=HIGHEST)
    elim = jnp.eye(SLOTS, dtype=F32) * live[:, None, :] - fitted
    crossy = jnp.einsum("aks,as->ak", masked, observed, precision=HIGHEST)
    solved = jnp.einsum("akl,al->ak", inverse, crossy, precision=HIGHEST)
    residual = live * (observed - jnp.einsum("aks,ak->as", block, solved, precision=HIGHEST))
    return elim, residual


def project(elim, rows):
    arcs = elim.shape[0]
    high = elim.astype(BF16)
    low = (elim - high.astype(F32)).astype(BF16)
    blocks = rows.reshape(arcs, SLOTS, rows.shape[1])
    dot = lambda a: jnp.einsum("ars,asc->arc", a, blocks, preferred_element_type=F32)
    return (dot(high) + dot(low)).astype(BF16).reshape(rows.shape)


def tdot(a, b):
    return lax.dot_general(a, b, (((0,), (0,)), ((), ())), preferred_element_type=F32)


def body(sizes, design, local, observed, valid, counts):
    nz, nyl, ncore, nx, nyh = sizes
    z, yl, core, x, yh = (lax.axis_index(name) for name in AXES)
    delta = (z - x) % nx
    half = design.shape[1] // 2
    top = design.shape[0] // 2
    down = [(i, (i - 1) % nx) for i in range(nx)]
    up = [(i, (i + 1) % nx) for i in range(nx)]
    swap = [(0, 1), (1, 0)]

    top1 = lax.ppermute(design[:top], "x", down)
    bot1 = lax.ppermute(design[top:], "x", up)
    flip = lax.ppermute(design, "yh", swap)
    top2 = lax.ppermute(top1, "x", down)
    bot2 = lax.ppermute(bot1, "x", up)

    live = live_rows(counts, valid)
    arcs = live.shape[0]
    elim, residual = eliminators(local, observed.reshape(live.shape), live)
    own = project(elim, design)
    rhs = jnp.dot(residual.reshape(1, -1), own.astype(F32), precision=HIGHEST)[0]
    rhs = lax.psum(rhs, ("z", "yl", "core"))

    def halves(a, cut):
        return jnp.where(cut == 1, jnp.concatenate([a[:, half:], a[:, :half]], 1), a)

    def core_sum(pieces):
        keep = lax.dynamic_index_in_dim(pieces, core, 0, False)
        send = lax.dynamic_index_in_dim(pieces, 1 - core, 0, False).astype(BF16)
        return keep + lax.ppermute(send, "core", swap).astype(F32)

    def z_sum(slots):
        total = lax.dynamic_index_in_dim(slots, delta, 0, False)
        for k in range(1, nz):
            send = lax.dynamic_index_in_dim(slots, (delta + k) % nz, 0, False).astype(BF16)
            got = lax.ppermute(send, "z", [(i, (i + k) % nz) for i in range(nz)])
            total = total + got.astype(F32)
        return total

    p_top1 = project(elim[: arcs // 2], top1)
    p_bot1 = project(elim[arcs // 2 :], bot1)
    early = jnp.stack([tdot(own, own), tdot(p_top1, own[:top]), tdot(p_bot1, own[top:])], 0)
    early = early.reshape(3, 2, half, 2 * half).transpose(1, 0, 2, 3)
    early = core_sum(early)
    early = jnp.stack([early[0], early[1], jnp.zeros_like(early[0]), early[2]])
    mine = z_sum(early)

    high = (x >= nx // 2).astype(jnp.int32)
    p_flip = project(elim, flip)
    p_two = jnp.concatenate([project(elim[: arcs // 2], top2), project(elim[arcs // 2 :], bot2)], 0)

    def quads(a, b):
        return jnp.stack([tdot(a[:, :half], b[:, :half]), tdot(a[:, half:], b[:, half:])])

    q_flip = quads(p_flip, halves(own, yh))
    q_two = quads(p_two, halves(own, high))
    q_far = quads(p_two, halves(p_flip, high))
    far_up = tdot(p_top1, p_flip[:top]).reshape(2, half, 2 * half)
    far_down = tdot(p_bot1, p_flip[top:]).reshape(2, half, 2 * half)
    late = jnp.stack(
        [
            jnp.concatenate([q_flip, jnp.zeros_like(q_flip)], 2),
            far_up,
            jnp.concatenate([q_two, q_far], 2),
            far_down,
        ],
        1,
    )
    late = z_sum(core_sum(late))

    same = yl == yh
    pad = jnp.zeros((half, half), F32)
    first = jnp.where(delta == 2, jnp.concatenate([late[:, :half], pad], 1), mine)
    second = jnp.where(delta == 2, jnp.concatenate([late[:, half:], pad], 1), late)
    got = lax.ppermute(jnp.where(same, second, first).astype(BF16), "yl", swap)
    total = jnp.where(same, first, second) + got.astype(F32)

    cut = jnp.where(delta == 2, high, yh)
    quad = jnp.logical_or(delta == 2, jnp.logical_and(delta == 0, jnp.logical_not(same)))
    right = (core ^ cut) == 1
    placed = jnp.where(jnp.logical_and(quad, right), jnp.concatenate([pad, total[:, :half]], 1), total)

    def index(a, k, b):
        return (a * ncore + k) * nx + b

    def column_half(a, k):
        return jnp.where(k == 1, a[:, half:], a[:, :half])

    mirrored = []
    for j in range(2):
        pairs = [
            (index(a, k, b), index(b, k ^ j, a))
            for a in range(nz)
            for k in range(ncore)
            for b in range(nx)
            if a != b
        ]
        send = column_half(placed, core ^ j).T.astype(BF16)
        mirrored.append(lax.ppermute(send, ("z", "core", "x"), pairs).astype(F32))
    left = jnp.where(core == 0, mirrored[0], mirrored[1])
    rest = jnp.where(core == 0, mirrored[1], mirrored[0])
    mirror = jnp.concatenate([left, rest], 1)

    def device(a, b, k, c, d):
        return (((a * nyl + b) * ncore + k) * nx + c) * nyh + d

    pairs = []
    for a in range(nz):
        for b in range(nyl):
            for k in range(ncore):
                for c in range(nx):
                    d = 1 - b
                    to = k ^ d if a == c else k
                    pairs.append((device(a, b, k, c, d), device(a, d, to, c, b)))
    on_diag = delta == 0
    send = jnp.where(on_diag, total, placed)
    across = lax.ppermute(send.astype(BF16), AXES, pairs).astype(F32)
    turned = across[:, :half].T
    turned = jnp.where(right, jnp.concatenate([turned, pad], 1), jnp.concatenate([pad, turned], 1))

    base = jnp.where(same, placed, across)
    out = jnp.where(on_diag, jnp.where(same, total, placed + turned), base + mirror)
    return out, rhs


def solution(mesh):
    sizes = (4, 2, 2, 4, 2)
    grid = Mesh(mesh.devices.reshape(sizes), AXES)
    arc, col = ("z", "yl", "core"), ("x", "yh")

    def run(design, local_design, observed, valid_mask, counts):
        return jax.shard_map(
            lambda *args: body(sizes, *args),
            mesh=grid,
            in_specs=(P(arc, col), P(None, arc), P(arc), P(arc), P(arc)),
            out_specs=(P(arc, col), P(col)),
            check_vma=False,
        )(design, local_design, observed, valid_mask, counts)

    return run
```

```python
import functools

import jax
import jax.numpy as jnp
from jax import lax
from jax.experimental import pallas as pl
from jax.experimental.pallas import tpu as pltpu
from jax.sharding import Mesh, PartitionSpec as P

LOCAL = 16
SLOTS = 192
AXES = ("z", "yl", "core", "x", "yh")
HIGHEST = lax.Precision.HIGHEST
F32 = jnp.float32
BF16 = jnp.bfloat16
VMEM = pl.BlockSpec(memory_space=pltpu.VMEM)
SMEM = pl.BlockSpec(memory_space=pltpu.SMEM)
PARAMS = pltpu.CompilerParams(vmem_limit_bytes=48 << 20)


def shape(dims, dtype):
    return jax.ShapeDtypeStruct(dims, dtype)


def inner(a, b, contract, precision=None):
    return lax.dot_general(a, b, ((contract[:1], contract[1:]), ((), ())), precision=precision, preferred_element_type=F32)


def iota(dims, axis):
    return lax.broadcasted_iota(jnp.int32, dims, axis)


def eliminate_kernel(counts, block, observed, valid, high, low, residual):
    arcs = block.shape[0]
    eye = (iota((LOCAL, LOCAL), 0) == iota((LOCAL, LOCAL), 1)).astype(F32)
    live, masked, grams = [], [], []
    for a in range(arcs):
        inside = (iota((1, SLOTS), 1) < counts[a]).astype(F32)
        live.append(inside * valid[a : a + 1, :].astype(F32))
        masked.append(block[a] * live[a])
        grams.append((inner(masked[a], block[a], (1, 1), HIGHEST) + eye)[None])
    gram = jnp.concatenate(grams, 0)
    rows, cols = iota(gram.shape, 1), iota(gram.shape, 2)
    for p in range(LOCAL):
        column = gram[:, :, p : p + 1]
        pivot = 1.0 / gram[:, p : p + 1, p : p + 1]
        row = gram[:, p : p + 1, :] * pivot
        swept = jnp.where(rows == p, row, gram - column * row)
        edge = jnp.where(rows == p, pivot, -column * pivot)
        gram = jnp.where(cols == p, edge, swept)
    diagonal = iota((SLOTS, SLOTS), 0) == iota((SLOTS, SLOTS), 1)
    for a in range(arcs):
        weights = jnp.dot(gram[a], masked[a], precision=HIGHEST, preferred_element_type=F32)
        fitted = inner(masked[a], weights, (0, 0), HIGHEST)
        elim = jnp.where(diagonal, live[a], 0.0) - fitted
        top = elim.astype(BF16)
        high[a * SLOTS : (a + 1) * SLOTS, :] = top
        low[a * SLOTS : (a + 1) * SLOTS, :] = (elim - top.astype(F32)).astype(BF16)
        y = observed[a : a + 1, :]
        solved = jnp.sum(weights * y, axis=1, keepdims=True)
        residual[a : a + 1, :] = live[a] * (y - jnp.sum(block[a] * solved, axis=0, keepdims=True))


def eliminate(local, observed, valid, counts):
    arcs = counts.shape[0]
    block = local.reshape(LOCAL, arcs, SLOTS).transpose(1, 0, 2)
    return pl.pallas_call(
        eliminate_kernel,
        out_shape=(
            shape((arcs * SLOTS, SLOTS), BF16),
            shape((arcs * SLOTS, SLOTS), BF16),
            shape((arcs, SLOTS), F32),
        ),
        in_specs=[SMEM, VMEM, VMEM, VMEM],
        out_specs=(VMEM, VMEM, VMEM),
        compiler_params=PARAMS,
        name="eliminate",
    )(counts, block, observed.reshape(arcs, SLOTS), valid.reshape(arcs, SLOTS))


def apply(high, low, rows):
    first = jnp.dot(high, rows, preferred_element_type=F32)
    return (first + jnp.dot(low, rows, preferred_element_type=F32)).astype(BF16)


def own_kernel(high, low, residual, rows, out, rhs):
    arc = pl.program_id(0)
    projected = apply(high[...], low[...], rows[...])
    out[...] = projected
    r = residual[pl.ds(arc, 1), :]
    one = r.astype(BF16).astype(F32)
    two = (r - one).astype(BF16).astype(F32)
    three = r - one - two
    parts = iota((16, SLOTS), 0)
    stack = jnp.where(parts == 0, one, jnp.where(parts == 1, two, jnp.where(parts == 2, three, 0.0)))
    part = jnp.dot(stack.astype(BF16), projected, preferred_element_type=F32)

    @pl.when(arc == 0)
    def _():
        rhs[...] = jnp.zeros_like(rhs)

    rhs[...] += jnp.sum(part, axis=0, keepdims=True)


def project_own(high, low, residual, rows):
    count, width = rows.shape
    arcs = count // SLOTS
    square = pl.BlockSpec((SLOTS, SLOTS), lambda i: (i, 0))
    wide = pl.BlockSpec((SLOTS, width), lambda i: (i, 0))
    return pl.pallas_call(
        own_kernel,
        grid=(arcs,),
        out_shape=(shape((count, width), BF16), shape((1, width), F32)),
        in_specs=[square, square, pl.BlockSpec((arcs, SLOTS), lambda i: (0, 0)), wide],
        out_specs=(wide, pl.BlockSpec((1, width), lambda i: (0, 0))),
        compiler_params=PARAMS,
        name="project_own",
    )(high, low, residual, rows)


def project_kernel(count, *refs):
    high, low = refs[:2]
    for i in range(count):
        top, bottom, out = refs[2 + 2 * i], refs[3 + 2 * i], refs[2 + 2 * count + i]
        out[0] = apply(high[0], low[0], top[...])
        out[1] = apply(high[1], low[1], bottom[...])


def project(high, low, pairs):
    rows, width = high.shape[0] // 2, pairs[0][0].shape[1]
    steps = rows // SLOTS
    square = pl.BlockSpec((2, SLOTS, SLOTS), lambda i: (0, i, 0))
    wide = pl.BlockSpec((SLOTS, width), lambda i: (i, 0))
    below = pl.BlockSpec((SLOTS, width), lambda i: (i + steps, 0))
    specs, args = [], []
    for top, bottom in pairs:
        args += [top, bottom]
        specs += [wide, below if bottom is top else wide]
    fold = lambda a: a.reshape(2, rows, SLOTS)
    outs = pl.pallas_call(
        functools.partial(project_kernel, len(pairs)),
        grid=(steps,),
        out_shape=[shape((2, rows, width), BF16)] * len(pairs),
        in_specs=[square, square] + specs,
        out_specs=[pl.BlockSpec((2, SLOTS, width), lambda i: (0, i, 0))] * len(pairs),
        compiler_params=PARAMS,
        name="project",
    )(fold(high), fold(low), *args)
    return [out.reshape(2 * rows, width) for out in outs]


def tdot(a, b):
    return inner(a, b, (0, 0))


def row_half(ref, which, half):
    return ref[pl.ds(pl.multiple_of(which * half, 8), half), :]


def early_send_kernel(half, where, a, b, c, out):
    other = 1 - where[0]
    for i, ref in enumerate((a, b, c)):
        out[i] = row_half(ref, other, half).astype(BF16)


def late_pieces(refs, which, half, store):
    flip, up, two, far, down = refs
    store(0, slice(0, half), flip[which])
    store(1, slice(0, 2 * half), row_half(up, which, half))
    store(2, slice(0, half), two[which])
    store(2, slice(half, 2 * half), far[which])
    store(3, slice(0, 2 * half), row_half(down, which, half))


def late_send_kernel(half, where, *refs):
    out = refs[-1]
    out[0, :, half:] = jnp.zeros((half, half), BF16)

    def store(slot, columns, value):
        out[slot, :, columns] = value.astype(BF16)

    late_pieces(refs[:-1], 1 - where[0], half, store)


def spread(where, sums, outs):
    delta = where[1]
    outs[0][...] = sums[delta]
    for k in range(1, 4):
        outs[k][...] = sums[(delta + k) % 4].astype(BF16)


def early_keep_kernel(half, where, a, b, c, got, mine, up1, up2, up3, sums):
    core = where[0]
    for i, (slot, ref) in enumerate(((0, a), (1, b), (3, c))):
        sums[slot] = row_half(ref, core, half) + got[i].astype(F32)
    sums[2] = jnp.zeros(sums.shape[1:], F32)
    spread(where, sums, (mine, up1, up2, up3))


def late_keep_kernel(half, where, *refs):
    got, mine, up1, up2, up3, sums = refs[-6:]
    sums[0, :, half:] = jnp.zeros((half, half), F32)

    def store(slot, columns, value):
        sums[slot, :, columns] = value + got[slot, :, columns].astype(F32)

    late_pieces(refs[:-6], where[0], half, store)
    spread(where, sums, (mine, up1, up2, up3))


def call(kernel, half, outs, where, *args, scratch=()):
    return pl.pallas_call(
        functools.partial(kernel, half),
        out_shape=outs,
        in_specs=[SMEM] + [VMEM] * len(args),
        out_specs=jax.tree.map(lambda _: VMEM, outs),
        scratch_shapes=scratch,
        compiler_params=PARAMS,
        name=kernel.__name__,
    )(where, *args)


def body(sizes, design, local, observed, valid, counts):
    nz, nyl, ncore, nx, nyh = sizes
    z, yl, core, x, yh = (lax.axis_index(name) for name in AXES)
    delta = (z - x) % nx
    half = design.shape[1] // 2
    top = design.shape[0] // 2
    down = [(i, (i - 1) % nx) for i in range(nx)]
    up = [(i, (i + 1) % nx) for i in range(nx)]
    swap = [(0, 1), (1, 0)]
    high_x = (x >= nx // 2).astype(jnp.int32)
    where = jnp.stack([core, delta]).astype(jnp.int32)

    flip = lax.ppermute(design, "yh", swap)
    top1 = lax.ppermute(design[:top], "x", down)
    bot1 = lax.ppermute(design[top:], "x", up)

    a_high, a_low, residual = eliminate(local, observed, valid, counts)
    own, rhs = project_own(a_high, a_low, residual, design)
    top1, bot1, own = lax.optimization_barrier((top1, bot1, own))
    top2 = lax.ppermute(top1, "x", down)
    bot2 = lax.ppermute(bot1, "x", up)

    rhs = rhs[0]
    rhs = rhs + lax.ppermute(rhs, "core", swap)
    rhs = rhs + lax.ppermute(rhs, "yl", swap)
    around = [lax.ppermute(rhs, "z", [(i, (i + k) % nz) for i in range(nz)]) for k in range(1, nz)]
    rhs = (rhs + around[1]) + (around[0] + around[2])

    def halves(a, cut):
        return jnp.where(cut == 1, jnp.concatenate([a[:, half:], a[:, :half]], 1), a)

    def over_z(mine, *sends):
        total = mine
        for k, send in enumerate(sends, 1):
            total = total + lax.ppermute(send, "z", [(i, (i + k) % nz) for i in range(nz)]).astype(F32)
        return total

    spread_outs = (shape((half, 2 * half), F32),) + (shape((half, 2 * half), BF16),) * 3
    sums = (pltpu.VMEM((nz, half, 2 * half), F32),)

    (p_one,) = project(a_high, a_low, [(top1, bot1)])
    p_top1, p_bot1 = p_one[:top], p_one[top:]
    early = [tdot(own, own), tdot(p_top1, own[:top]), tdot(p_bot1, own[top:])]
    send = call(early_send_kernel, half, shape((3, half, 2 * half), BF16), where, *early)
    got = lax.ppermute(send, "core", swap)
    spread_early = call(early_keep_kernel, half, spread_outs, where, *early, got, scratch=sums)
    mine = over_z(*spread_early)

    flip, top2, bot2 = lax.optimization_barrier((flip, top2, bot2, spread_early))[:3]
    p_flip, p_two = project(a_high, a_low, [(flip, flip), (top2, bot2)])

    def quads(a, b):
        return jnp.stack([tdot(a[:, :half], b[:, :half]), tdot(a[:, half:], b[:, half:])])

    late = [
        quads(p_flip, halves(own, yh)),
        tdot(p_top1, p_flip[:top]),
        quads(p_two, halves(own, high_x)),
        quads(p_two, halves(p_flip, high_x)),
        tdot(p_bot1, p_flip[top:]),
    ]
    send = call(late_send_kernel, half, shape((4, half, 2 * half), BF16), where, *late)
    got = lax.ppermute(send, "core", swap)
    spread_late = call(late_keep_kernel, half, spread_outs, where, *late, got, scratch=sums)
    late = over_z(*spread_late)

    same = yl == yh
    pad = jnp.zeros((half, half), F32)
    first = jnp.where(delta == 2, jnp.concatenate([late[:, :half], pad], 1), mine)
    second = jnp.where(delta == 2, jnp.concatenate([late[:, half:], pad], 1), late)
    got = lax.ppermute(jnp.where(same, second, first).astype(BF16), "yl", swap)
    total = jnp.where(same, first, second) + got.astype(F32)

    cut = jnp.where(delta == 2, high_x, yh)
    quad = jnp.logical_or(delta == 2, jnp.logical_and(delta == 0, jnp.logical_not(same)))
    right = (core ^ cut) == 1
    placed = jnp.where(jnp.logical_and(quad, right), jnp.concatenate([pad, total[:, :half]], 1), total)

    def index(a, k, b):
        return (a * ncore + k) * nx + b

    def column_half(a, k):
        return jnp.where(k == 1, a[:, half:], a[:, :half])

    mirrored = []
    for j in range(2):
        pairs = [
            (index(a, k, b), index(b, k ^ j, a))
            for a in range(nz)
            for k in range(ncore)
            for b in range(nx)
            if a != b
        ]
        send = column_half(placed, core ^ j).T.astype(BF16)
        mirrored.append(lax.ppermute(send, ("z", "core", "x"), pairs).astype(F32))
    left = jnp.where(core == 0, mirrored[0], mirrored[1])
    rest = jnp.where(core == 0, mirrored[1], mirrored[0])
    mirror = jnp.concatenate([left, rest], 1)

    def device(a, b, k, c, d):
        return (((a * nyl + b) * ncore + k) * nx + c) * nyh + d

    pairs = []
    for a in range(nz):
        for b in range(nyl):
            for k in range(ncore):
                for c in range(nx):
                    d = 1 - b
                    to = k ^ d if a == c else k
                    pairs.append((device(a, b, k, c, d), device(a, d, to, c, b)))
    on_diag = delta == 0
    send = jnp.where(on_diag, total, placed)
    across = lax.ppermute(send.astype(BF16), AXES, pairs).astype(F32)
    turned = across[:, :half].T
    turned = jnp.where(right, jnp.concatenate([turned, pad], 1), jnp.concatenate([pad, turned], 1))

    base = jnp.where(same, placed, across)
    out = jnp.where(on_diag, jnp.where(same, total, placed + turned), base + mirror)
    return out, rhs


def solution(mesh):
    sizes = (4, 2, 2, 4, 2)
    grid = Mesh(mesh.devices.reshape(sizes), AXES)
    arc, col = ("z", "yl", "core"), ("x", "yh")

    def run(design, local_design, observed, valid_mask, counts):
        return jax.shard_map(
            functools.partial(body, sizes),
            mesh=grid,
            in_specs=(P(arc, col), P(None, arc), P(arc), P(arc), P(arc)),
            out_specs=(P(arc, col), P(col)),
            check_vma=False,
        )(design, local_design, observed, valid_mask, counts)

    return run
```

```python
import functools

import jax
import jax.numpy as jnp
from jax import lax
from jax.experimental import pallas as pl
from jax.experimental.pallas import tpu as pltpu
from jax.sharding import Mesh, PartitionSpec as P

LOCAL = 16
SLOTS = 192
AXES = ("z", "yl", "core", "x", "yh")
HIGHEST = lax.Precision.HIGHEST
F32 = jnp.float32
BF16 = jnp.bfloat16
VMEM = pl.BlockSpec(memory_space=pltpu.VMEM)
SMEM = pl.BlockSpec(memory_space=pltpu.SMEM)
PARAMS = pltpu.CompilerParams(vmem_limit_bytes=48 << 20)
CHEAP = pl.CostEstimate(flops=1, transcendentals=0, bytes_accessed=1)


def shape(dims, dtype):
    return jax.ShapeDtypeStruct(dims, dtype)


def inner(a, b, contract, precision=None):
    return lax.dot_general(a, b, ((contract[:1], contract[1:]), ((), ())), precision=precision, preferred_element_type=F32)


def iota(dims, axis):
    return lax.broadcasted_iota(jnp.int32, dims, axis)


def eliminate_kernel(counts, block, observed, valid, high, low, residual):
    arcs = block.shape[0]
    eye = (iota((LOCAL, LOCAL), 0) == iota((LOCAL, LOCAL), 1)).astype(F32)
    live, masked, grams = [], [], []
    for a in range(arcs):
        inside = (iota((1, SLOTS), 1) < counts[a]).astype(F32)
        live.append(inside * valid[a : a + 1, :].astype(F32))
        masked.append(block[a] * live[a])
        grams.append((inner(masked[a], block[a], (1, 1), HIGHEST) + eye)[None])
    gram = jnp.concatenate(grams, 0)
    rows, cols = iota(gram.shape, 1), iota(gram.shape, 2)
    for p in range(LOCAL):
        column = gram[:, :, p : p + 1]
        pivot = 1.0 / gram[:, p : p + 1, p : p + 1]
        row = gram[:, p : p + 1, :] * pivot
        swept = jnp.where(rows == p, row, gram - column * row)
        edge = jnp.where(rows == p, pivot, -column * pivot)
        gram = jnp.where(cols == p, edge, swept)
    diagonal = iota((SLOTS, SLOTS), 0) == iota((SLOTS, SLOTS), 1)
    for a in range(arcs):
        weights = jnp.dot(gram[a], masked[a], precision=HIGHEST, preferred_element_type=F32)
        fitted = inner(masked[a], weights, (0, 0), HIGHEST)
        elim = jnp.where(diagonal, live[a], 0.0) - fitted
        top = elim.astype(BF16)
        high[a * SLOTS : (a + 1) * SLOTS, :] = top
        low[a * SLOTS : (a + 1) * SLOTS, :] = (elim - top.astype(F32)).astype(BF16)
        y = observed[a : a + 1, :]
        solved = jnp.sum(weights * y, axis=1, keepdims=True)
        residual[a : a + 1, :] = live[a] * (y - jnp.sum(block[a] * solved, axis=0, keepdims=True))


def eliminate(local, observed, valid, counts):
    arcs = counts.shape[0]
    block = local.reshape(LOCAL, arcs, SLOTS).transpose(1, 0, 2)
    return pl.pallas_call(
        eliminate_kernel,
        out_shape=(
            shape((arcs * SLOTS, SLOTS), BF16),
            shape((arcs * SLOTS, SLOTS), BF16),
            shape((arcs, SLOTS), F32),
        ),
        in_specs=[SMEM, VMEM, VMEM, VMEM],
        out_specs=(VMEM, VMEM, VMEM),
        compiler_params=PARAMS,
        cost_estimate=CHEAP,
        name="eliminate",
    )(counts, block, observed.reshape(arcs, SLOTS), valid.reshape(arcs, SLOTS))


def rounded(high, low, rows):
    first = jnp.dot(high, rows, preferred_element_type=F32)
    return (first + jnp.dot(low, rows, preferred_element_type=F32)).astype(BF16)


def project_into(out, high, low, rows, begin, count, source):
    for i in range(count):
        to = slice((begin + i) * SLOTS, (begin + i + 1) * SLOTS)
        at = slice((source + i) * SLOTS, (source + i + 1) * SLOTS)
        out[to, :] = rounded(high[to, :], low[to, :], rows[at, :])


def own_kernel(high, low, residual, rows, out, product, rhs):
    arcs = residual.shape[0]
    half = product.shape[1]
    project_into(out, high, low, rows, 0, arcs, 0)
    total = jnp.zeros((1, rows.shape[1]), F32)
    parts = iota((16, SLOTS), 0)
    for a in range(arcs):
        r = residual[a : a + 1, :]
        one = r.astype(BF16).astype(F32)
        two = (r - one).astype(BF16).astype(F32)
        three = r - one - two
        stack = jnp.where(parts == 0, one, jnp.where(parts == 1, two, jnp.where(parts == 2, three, 0.0)))
        part = jnp.dot(stack.astype(BF16), out[a * SLOTS : (a + 1) * SLOTS, :], preferred_element_type=F32)
        total = total + jnp.sum(part, axis=0, keepdims=True)
    rhs[...] = total
    result = tdot(out[...], out[...])
    product[0] = result[:half]
    product[1] = result[half:]


def near_kernel(where, high, low, own, product, above, below, out, both, send):
    arcs, half = high.shape[0] // SLOTS, product.shape[1]
    top = above.shape[0]
    project_into(out, high, low, above, 0, arcs // 2, 0)
    project_into(out, high, low, below, arcs // 2, arcs // 2, 0)
    for piece, rows in enumerate((slice(0, top), slice(top, 2 * top))):
        result = tdot(out[rows, :], own[rows, :])
        both[0, piece] = result[:half]
        both[1, piece] = result[half:]
    other = 1 - where[0]
    send[0] = product[other].astype(BF16)
    send[1] = both[other, 0].astype(BF16)
    send[2] = both[other, 1].astype(BF16)


def far_kernel(where, high, low, own, near, flip_top, flip_bottom, above, below, both, send, flip, two):
    arcs, half = high.shape[0] // SLOTS, both.shape[2]
    top = above.shape[0]
    project_into(flip, high, low, flip_top, 0, arcs // 2, 0)
    project_into(flip, high, low, flip_bottom, arcs // 2, arcs // 2, 0)
    project_into(two, high, low, above, 0, arcs // 2, 0)
    project_into(two, high, low, below, arcs // 2, arcs // 2, 0)
    for slot, rows in ((1, slice(0, top)), (3, slice(top, 2 * top))):
        result = tdot(near[rows, :], flip[rows, :])
        both[0, slot] = result[:half]
        both[1, slot] = result[half:]
    cut_flip, cut_two = where[2], where[3]

    def quadrants(a, b, cut, slot, columns):
        result = tdot(a[...], b[...])
        for r in range(2):
            rows = result[r * half : (r + 1) * half]
            both[r, slot, :, columns] = jnp.where(cut == r, rows[:, :half], rows[:, half:])

    for r in range(2):
        both[r, 0, :, half:] = jnp.zeros((half, half), F32)
    quadrants(flip, own, cut_flip, 0, slice(0, half))
    quadrants(two, own, cut_two, 2, slice(0, half))
    quadrants(two, flip, cut_two, 2, slice(half, 2 * half))
    send[...] = both[1 - where[0]].astype(BF16)


def tdot(a, b):
    return inner(a, b, (0, 0))


def spread(where, sums, mine, ups):
    delta = where[1]
    mine[...] = sums[delta]
    for k, up in enumerate(ups, 1):
        up[...] = sums[(delta + k) % 4].astype(BF16)


def near_spread_kernel(where, product, both, got, mine, up1, up2, up3, sums):
    core = where[0]
    sums[0] = product[core] + got[0].astype(F32)
    sums[1] = both[core, 0] + got[1].astype(F32)
    sums[2] = jnp.zeros(sums.shape[1:], F32)
    sums[3] = both[core, 1] + got[2].astype(F32)
    spread(where, sums, mine, (up1, up2, up3))


def far_spread_kernel(where, both, got, mine, up1, up2, up3, sums):
    sums[...] = both[where[0]] + got[...].astype(F32)
    spread(where, sums, mine, (up1, up2, up3))


def near_total_kernel(mine, one, two, three, total, send):
    total[...] = ((mine[...] + one[...].astype(F32)) + two[...].astype(F32)) + three[...].astype(F32)
    send[...] = total[...].astype(BF16)


def far_total_kernel(where, mine, one, two, three, keep, send):
    total = ((mine[...] + one[...].astype(F32)) + two[...].astype(F32)) + three[...].astype(F32)
    half = total.shape[0]
    opposite, same = where[1] == 2, where[4] == 1
    turned = jnp.concatenate([total[:, half:], total[:, :half]], 1)
    send[...] = jnp.where(jnp.logical_and(opposite, same), turned, total).astype(BF16)
    keep[...] = jnp.where(jnp.logical_and(opposite, jnp.logical_not(same)), turned, total)


def place_kernel(where, near, near_got, keep, got, placed, first, second, across):
    half = placed.shape[0]
    core, delta, same, right = where[0], where[1], where[4] == 1, where[5] == 1
    late = keep[...] + got[...].astype(F32)
    early = near[...] + near_got[...].astype(F32)
    total = jnp.where(jnp.logical_and(same, delta != 2), early, late)
    quad = jnp.logical_or(delta == 2, jnp.logical_and(delta == 0, jnp.logical_not(same)))
    left_side = jnp.where(jnp.logical_and(quad, right), 0.0, total[:, :half])
    right_side = jnp.where(quad, jnp.where(right, total[:, :half], 0.0), total[:, half:])
    placed[:, :half] = left_side
    placed[:, half:] = right_side
    low, high = left_side.astype(BF16), right_side.astype(BF16)
    first[...] = jnp.where(core == 0, low, high)
    second[...] = jnp.where(core == 0, high, low)
    diagonal = delta == 0
    across[:, :half] = jnp.where(diagonal, total[:, :half].astype(BF16), low)
    across[:, half:] = high


def finish_kernel(where, placed, first, second, across, out):
    half = out.shape[0]
    core, delta, same, right = where[0], where[1], where[4] == 1, where[5] == 1
    one, two = first[...].astype(F32), second[...].astype(F32)
    quad = across[:, :half].astype(F32)
    diagonal = delta == 0
    left = jnp.where(diagonal, jnp.where(right, quad, 0.0), jnp.where(core == 0, one, two))
    rest = jnp.where(diagonal, jnp.where(right, 0.0, quad), jnp.where(core == 0, two, one))
    keep = jnp.logical_or(diagonal, same)
    out[:, :half] = jnp.where(keep, placed[:, :half], quad) + left.T
    out[:, half:] = jnp.where(keep, placed[:, half:], across[:, half:].astype(F32)) + rest.T


def call(kernel, outs, *args, scalars=True, scratch=()):
    return pl.pallas_call(
        kernel,
        out_shape=outs,
        in_specs=[SMEM if scalars and i == 0 else VMEM for i in range(len(args))],
        out_specs=jax.tree.map(lambda _: VMEM, outs),
        scratch_shapes=scratch,
        compiler_params=PARAMS,
        cost_estimate=CHEAP,
        name=kernel.__name__,
    )(*args)


def body(sizes, design, local, observed, valid, counts):
    nz, nyl, ncore, nx, nyh = sizes
    z, yl, core, x, yh = (lax.axis_index(name) for name in AXES)
    delta = (z - x) % nx
    rows, width = design.shape
    half, top = width // 2, rows // 2
    down = [(i, (i - 1) % nx) for i in range(nx)]
    up = [(i, (i + 1) % nx) for i in range(nx)]
    swap = [(0, 1), (1, 0)]
    turn = lambda k: [(i, (i + k) % nz) for i in range(nz)]
    high_x = (x >= nx // 2).astype(jnp.int32)
    same = (yl == yh).astype(jnp.int32)
    right = core ^ jnp.where(delta == 2, high_x, yh)
    where = jnp.stack([core, delta, yh, high_x, same, right]).astype(jnp.int32)

    upper, lower = design[:top], design[top:]
    above = lax.ppermute(upper, "x", down)
    below = lax.ppermute(lower, "x", up)
    flip_top = lax.ppermute(upper, "yh", swap)

    a_high, a_low, residual = eliminate(local, observed, valid, counts)
    own, product, rhs = call(
        own_kernel,
        (shape((rows, width), BF16), shape((2, half, width), F32), shape((1, width), F32)),
        a_high, a_low, residual, design,
        scalars=False,
    )
    rhs = rhs[0]
    rhs = rhs + lax.ppermute(rhs, "core", swap)
    rhs = rhs + lax.ppermute(rhs, "yl", swap)
    around = [lax.ppermute(rhs, "z", turn(k)) for k in range(1, nz)]
    rhs = (rhs + around[1]) + (around[0] + around[2])

    above, below, flip_top, own, lower, rhs = lax.optimization_barrier((above, below, flip_top, own, lower, rhs))
    flip_bottom = lax.ppermute(lower, "yh", swap)
    above2 = lax.ppermute(above, "x", down)
    below2 = lax.ppermute(below, "x", up)

    wide, sent = shape((half, width), F32), shape((half, width), BF16)
    sums = (pltpu.VMEM((nz, half, width), F32),)

    near, both, send = call(
        near_kernel,
        (shape((rows, width), BF16), shape((2, 2, half, width), F32), shape((3, half, width), BF16)),
        where, a_high, a_low, own, product, above, below,
    )
    got = lax.ppermute(send, "core", swap)
    mine, *ups = call(near_spread_kernel, (wide, sent, sent, sent), where, product, both, got, scratch=sums)
    ups = [lax.ppermute(v, "z", turn(k)) for k, v in enumerate(ups, 1)]
    early, send = call(near_total_kernel, (wide, sent), mine, *ups, scalars=False)

    flip_top, flip_bottom, above2, below2, early, send = lax.optimization_barrier(
        (flip_top, flip_bottom, above2, below2, early, send)
    )
    early_got = lax.ppermute(send, ("yl", "yh"), [(1, 3), (2, 0)])
    both, send = call(
        far_kernel,
        (shape((2, nz, half, width), F32), shape((nz, half, width), BF16)),
        where, a_high, a_low, own, near, flip_top, flip_bottom, above2, below2,
        scratch=(pltpu.VMEM((rows, width), BF16), pltpu.VMEM((rows, width), BF16)),
    )
    got = lax.ppermute(send, "core", swap)
    mine, *ups = call(far_spread_kernel, (wide, sent, sent, sent), where, both, got, scratch=sums)
    ups = [lax.ppermute(v, "z", turn(k)) for k, v in enumerate(ups, 1)]
    keep, send = call(far_total_kernel, (wide, sent), where, mine, *ups)
    got = lax.ppermute(send, "yl", swap)

    quad = shape((half, half), BF16)
    placed, first, second, across = call(
        place_kernel, (wide, quad, quad, sent), where, early, early_got, keep, got
    )

    def index(a, k, b):
        return (a * ncore + k) * nx + b

    turned = []
    for j, send in enumerate((first, second)):
        pairs = [
            (index(a, k, b), index(b, k ^ j, a))
            for a in range(nz)
            for k in range(ncore)
            for b in range(nx)
            if a != b and ((a - b) % nx != 2 or (b >= nx // 2) == (j == 1))
        ]
        turned.append(lax.ppermute(send, ("z", "core", "x"), pairs))

    def device(a, b, k, c, d):
        return (((a * nyl + b) * ncore + k) * nx + c) * nyh + d

    pairs = []
    for a in range(nz):
        for b in range(nyl):
            for k in range(ncore):
                for c in range(nx):
                    d = 1 - b
                    to = k ^ d if a == c else k
                    pairs.append((device(a, b, k, c, d), device(a, d, to, c, b)))
    across = lax.ppermute(across, AXES, pairs)
    out = call(finish_kernel, wide, where, placed, *turned, across)
    return out, rhs


def solution(mesh):
    sizes = (4, 2, 2, 4, 2)
    grid = Mesh(mesh.devices.reshape(sizes), AXES)
    arc, col = ("z", "yl", "core"), ("x", "yh")

    def run(design, local_design, observed, valid_mask, counts):
        return jax.shard_map(
            functools.partial(body, sizes),
            mesh=grid,
            in_specs=(P(arc, col), P(None, arc), P(arc), P(arc), P(arc)),
            out_specs=(P(arc, col), P(col)),
            check_vma=False,
        )(design, local_design, observed, valid_mask, counts)

    return run
```

```python
import functools

import jax
import jax.numpy as jnp
from jax import lax
from jax.experimental import pallas as pl
from jax.experimental.pallas import tpu as pltpu
from jax.sharding import Mesh, PartitionSpec as P

LOCAL = 16
SLOTS = 192
AXES = ("z", "yl", "core", "x", "yh")
HIGHEST = lax.Precision.HIGHEST
F32 = jnp.float32
BF16 = jnp.bfloat16
VMEM = pl.BlockSpec(memory_space=pltpu.VMEM)
SMEM = pl.BlockSpec(memory_space=pltpu.SMEM)
PARAMS = pltpu.CompilerParams(vmem_limit_bytes=16 << 20)
CHEAP = pl.CostEstimate(flops=1, transcendentals=0, bytes_accessed=1)


def shape(dims, dtype):
    return jax.ShapeDtypeStruct(dims, dtype)


def inner(a, b, contract, precision=None):
    return lax.dot_general(a, b, ((contract[:1], contract[1:]), ((), ())), precision=precision, preferred_element_type=F32)


def iota(dims, axis):
    return lax.broadcasted_iota(jnp.int32, dims, axis)


def eliminate_kernel(counts, block, observed, valid, high, low, residual):
    arcs = block.shape[0]
    eye = (iota((LOCAL, LOCAL), 0) == iota((LOCAL, LOCAL), 1)).astype(F32)
    live, masked, grams = [], [], []
    for a in range(arcs):
        inside = (iota((1, SLOTS), 1) < counts[a]).astype(F32)
        live.append(inside * valid[a : a + 1, :].astype(F32))
        masked.append(block[a] * live[a])
        grams.append((inner(masked[a], block[a], (1, 1), HIGHEST) + eye)[None])
    gram = jnp.concatenate(grams, 0)
    rows, cols = iota(gram.shape, 1), iota(gram.shape, 2)
    for p in range(LOCAL):
        column = gram[:, :, p : p + 1]
        pivot = 1.0 / gram[:, p : p + 1, p : p + 1]
        row = gram[:, p : p + 1, :] * pivot
        swept = jnp.where(rows == p, row, gram - column * row)
        edge = jnp.where(rows == p, pivot, -column * pivot)
        gram = jnp.where(cols == p, edge, swept)
    diagonal = iota((SLOTS, SLOTS), 0) == iota((SLOTS, SLOTS), 1)
    for a in range(arcs):
        weights = jnp.dot(gram[a], masked[a], precision=HIGHEST, preferred_element_type=F32)
        fitted = inner(masked[a], weights, (0, 0), HIGHEST)
        elim = jnp.where(diagonal, live[a], 0.0) - fitted
        top = elim.astype(BF16)
        high[a * SLOTS : (a + 1) * SLOTS, :] = top
        low[a * SLOTS : (a + 1) * SLOTS, :] = (elim - top.astype(F32)).astype(BF16)
        y = observed[a : a + 1, :]
        solved = jnp.sum(weights * y, axis=1, keepdims=True)
        residual[a : a + 1, :] = live[a] * (y - jnp.sum(block[a] * solved, axis=0, keepdims=True))


def eliminate(local, observed, valid, counts):
    arcs = counts.shape[0]
    block = local.reshape(LOCAL, arcs, SLOTS).transpose(1, 0, 2)
    return pl.pallas_call(
        eliminate_kernel,
        out_shape=(
            shape((arcs * SLOTS, SLOTS), BF16),
            shape((arcs * SLOTS, SLOTS), BF16),
            shape((arcs, SLOTS), F32),
        ),
        in_specs=[SMEM, VMEM, VMEM, VMEM],
        out_specs=(VMEM, VMEM, VMEM),
        compiler_params=PARAMS,
        cost_estimate=CHEAP,
        name="eliminate",
    )(counts, block, observed.reshape(arcs, SLOTS), valid.reshape(arcs, SLOTS))


def rounded(high, low, rows):
    first = jnp.dot(high, rows, preferred_element_type=F32)
    return (first + jnp.dot(low, rows, preferred_element_type=F32)).astype(BF16)


def project_into(out, high, low, rows, begin, count, source):
    for i in range(count):
        to = slice((begin + i) * SLOTS, (begin + i + 1) * SLOTS)
        at = slice((source + i) * SLOTS, (source + i + 1) * SLOTS)
        out[to, :] = rounded(high[to, :], low[to, :], rows[at, :])


def project_half(out, high, low, rows, first, count):
    for i in range(count):
        at = slice(i * SLOTS, (i + 1) * SLOTS)
        arc = slice((first + i) * SLOTS, (first + i + 1) * SLOTS)
        out[at, :] = rounded(high[arc, :], low[arc, :], rows[at, :])


def split(core, result, keep, send):
    half = result.shape[0] // 2
    keep[...] = jnp.where(core == 0, result[:half], result[half:])
    send[...] = jnp.where(core == 0, result[half:], result[:half]).astype(BF16)


def parts_of(value):
    one = value.astype(BF16).astype(F32)
    two = (value - one).astype(BF16).astype(F32)
    three = value - one - two
    line = iota((16, value.shape[1]), 0)
    stack = jnp.where(line == 0, one, jnp.where(line == 1, two, jnp.where(line == 2, three, 0.0)))
    return stack.astype(BF16)


def whole_of(block):
    parts = block.astype(F32)
    return (parts[0:1] + parts[1:2]) + parts[2:3]


def own_kernel(where, high, low, residual, rows, out, turned, keep, send, rhs):
    arcs, half = residual.shape[0], keep.shape[0]
    project_into(out, high, low, rows, 0, arcs, 0)
    total = jnp.zeros((1, rows.shape[1]), F32)
    for a in range(arcs):
        stack = parts_of(residual[a : a + 1, :])
        part = jnp.dot(stack, out[a * SLOTS : (a + 1) * SLOTS, :], preferred_element_type=F32)
        total = total + jnp.sum(part, axis=0, keepdims=True)
    rhs[...] = total
    send[half:, :] = parts_of(total)
    turned[...] = out[...].T
    result = jnp.dot(turned[...], out[...], preferred_element_type=F32)
    split(where[0], result, keep, send.at[pl.ds(0, half), :])


def near_kernel(where, high, low, own, above, below, near_top, near_bottom, keep, send):
    arcs = high.shape[0] // SLOTS
    top = above.shape[0]
    project_half(near_top, high, low, above, 0, arcs // 2)
    project_half(near_bottom, high, low, below, arcs // 2, arcs // 2)
    for piece, near in enumerate((near_top, near_bottom)):
        result = jnp.dot(own[:, piece * top : (piece + 1) * top], near[...], preferred_element_type=F32)
        split(where[0], result, keep.at[piece], send.at[piece])


def middle_kernel(where, high, low, near, rows, flip, turned, keep, send):
    top = rows.shape[0]
    project_into(flip, high, low, rows, 0, top // SLOTS, 0)
    turned[...] = flip[...].T
    split(where[0], jnp.dot(turned[...], near[...], preferred_element_type=F32), keep, send)


def far_rows(where, chunk, own, near, done, done_send, flips, turned, two, keep, send):
    size, half = keep.shape[1], own.shape[0] // 2
    top = two.shape[0] // 2
    core, cut_flip, cut_two = where[0], where[2], where[3]
    upper, lower = slice(0, top), slice(top, 2 * top)
    rows = slice(chunk * size, (chunk + 1) * size)

    def lines(ref):
        return jnp.concatenate([ref[rows, :], ref[half + chunk * size : half + (chunk + 1) * size, :]], 0)

    def times(a, b):
        return jnp.dot(a, b, preferred_element_type=F32)

    own_lines, flip_top, flip_bottom = lines(own), lines(turned[0]), lines(turned[1])
    keep[1] = done[rows, :]
    send[1] = done_send[rows, :]
    split(core, times(flip_bottom, near[...]), keep.at[3], send.at[3])

    def quadrants(result, cut, slot, columns):
        first = jnp.where(cut == 0, result[:size, :half], result[:size, half:])
        second = jnp.where(cut == 1, result[size:, :half], result[size:, half:])
        keep[slot, :, columns] = jnp.where(core == 0, first, second)
        send[slot, :, columns] = jnp.where(core == 0, second, first).astype(BF16)

    quadrants(
        times(own_lines[:, upper], flips[0][...]) + times(own_lines[:, lower], flips[1][...]),
        cut_flip, 0, slice(0, half),
    )
    keep[0, :, half:] = jnp.zeros((size, half), F32)
    send[0, :, half:] = jnp.zeros((size, half), BF16)
    quadrants(times(own_lines, two[...]), cut_two, 2, slice(0, half))
    quadrants(
        times(flip_top, two[upper, :]) + times(flip_bottom, two[lower, :]),
        cut_two, 2, slice(half, 2 * half),
    )


def far_kernel(
    where, high, low, own, near, done, done_send, flip_top, top_turned, rows, above, below,
    keep, send, flip_bottom, bottom_turned, two,
):
    arcs = high.shape[0] // SLOTS
    project_half(flip_bottom, high, low, rows, arcs // 2, arcs // 2)
    bottom_turned[...] = flip_bottom[...].T
    project_into(two, high, low, above, 0, arcs // 2, 0)
    project_into(two, high, low, below, arcs // 2, arcs // 2, 0)
    flips, turned = (flip_top, flip_bottom), (top_turned, bottom_turned)
    far_rows(where, 0, own, near, done, done_send, flips, turned, two, keep, send)


def far_rest_kernel(
    where, own, near, done, done_send, flip_top, top_turned, flip_bottom, bottom_turned, two, keep, send
):
    flips, turned = (flip_top, flip_bottom), (top_turned, bottom_turned)
    far_rows(where, 1, own, near, done, done_send, flips, turned, two, keep, send)


def tdot(a, b):
    return inner(a, b, (0, 0))


def spread(where, sums, mine, ups):
    delta = where[1]
    mine[...] = sums[delta]
    for k, up in enumerate(ups, 1):
        up[...] = sums[(delta + k) % 4].astype(BF16)


def near_spread_kernel(where, own, keep, rhs, own_got, got, mine, up1, up2, up3, rhs_sum, sums):
    half = own.shape[0]
    sums[0] = own[...] + own_got[:half, :].astype(F32)
    sums[1] = keep[0] + got[0].astype(F32)
    sums[2] = jnp.zeros(sums.shape[1:], F32)
    sums[3] = keep[1] + got[1].astype(F32)
    spread(where, sums, mine, (up1, up2, up3))
    rhs_sum[...] = rhs[...] + whole_of(own_got[half:, :])


def far_spread_kernel(where, keep, got, rhs, mine, up1, up2, up3):
    delta, size = where[1], keep.shape[1]
    mine[...] = keep[delta] + got[delta].astype(F32)
    for k, up in enumerate((up1, up2, up3), 1):
        slot = (delta + k) % 4
        up[:size, :] = (keep[slot] + got[slot].astype(F32)).astype(BF16)
        if up.shape[0] > size:
            up[size:, :] = parts_of(rhs[...])


def near_total_kernel(mine, one, two, three, total, send):
    total[...] = ((mine[...] + one[...].astype(F32)) + two[...].astype(F32)) + three[...].astype(F32)
    send[...] = total[...].astype(BF16)


def far_total_kernel(where, rhs, *refs):
    keep, send, rhs_sum = refs[-3:]
    half = keep.shape[0]
    opposite, same = where[1] == 2, where[4] == 1
    first = 0
    for chunk in range(len(refs) // 4):
        mine, one, two, three = refs[4 * chunk : 4 * chunk + 4]
        size = mine.shape[0]
        one, two, three = (up[:size, :].astype(F32) for up in (one, two, three))
        total = ((mine[...] + one) + two) + three
        rows = slice(first, first + size)
        first += size
        turned = jnp.concatenate([total[:, half:], total[:, :half]], 1)
        send[rows, :] = jnp.where(jnp.logical_and(opposite, same), turned, total).astype(BF16)
        keep[rows, :] = jnp.where(jnp.logical_and(opposite, jnp.logical_not(same)), turned, total)
    one, two, three = (whole_of(up[refs[0].shape[0] :, :]) for up in refs[1:4])
    total = (rhs[...] + two) + (one + three)
    rhs_sum[...] = total
    send[half:, :] = parts_of(total)


def place_kernel(where, near, near_got, keep, got, rhs, placed, mirror, mirror_quad, quad_send, rhs_sum):
    half = placed.shape[0]
    core, delta, same, right = where[0], where[1], where[4] == 1, where[5] == 1
    late = keep[...] + got[:half, :].astype(F32)
    early = near[...] + near_got[...].astype(F32)
    total = jnp.where(jnp.logical_and(same, delta != 2), early, late)
    quad = jnp.logical_or(delta == 2, jnp.logical_and(delta == 0, jnp.logical_not(same)))
    left_side = jnp.where(jnp.logical_and(quad, right), 0.0, total[:, :half])
    right_side = jnp.where(quad, jnp.where(right, total[:, :half], 0.0), total[:, half:])
    placed[:, :half] = left_side
    placed[:, half:] = right_side
    mirror[...] = placed[...].astype(BF16)
    mirror_quad[...] = total[:, :half].astype(BF16)
    quad_send[...] = jnp.where(core == 0, right_side, left_side).astype(BF16)
    rhs_sum[...] = rhs[...] + whole_of(got[half:, :])


def turn_kernel(where, placed, got, turned, across):
    half = placed.shape[0]
    core, diagonal = where[0], where[1] == 0
    mine = jnp.where(core == 0, placed[:, :half], placed[:, half:])
    other = got[...].astype(F32)
    first = jnp.where(core == 0, mine, other).T
    second = jnp.where(core == 0, other, mine).T
    turned[:, :half] = first
    turned[:, half:] = second
    across[...] = jnp.where(diagonal, placed[...], turned[...]).astype(BF16)


def finish_kernel(where, placed, turned, mirror, mirror_quad, across, out):
    half = out.shape[0]
    diagonal, opposite, same = where[1] == 0, where[1] == 2, where[4] == 1
    left = where[5] == 1
    for side, columns in enumerate((slice(0, half), slice(half, 2 * half))):
        far = across[:, columns].astype(F32)
        quad = jnp.where(left == (side == 0), mirror_quad[...].astype(F32), 0.0)
        near = jnp.where(opposite, quad, mirror[:, columns].astype(F32))
        own = turned[:, columns]
        direct = jnp.where(diagonal, jnp.where(same, placed[:, columns], far), near)
        other = jnp.where(diagonal, jnp.where(same, 0.0, own), jnp.where(same, own, far))
        out[:, columns] = direct + other


def call(kernel, outs, *args, scalars=True, scratch=(), vmem=12):
    return pl.pallas_call(
        kernel,
        out_shape=outs,
        in_specs=[SMEM if scalars and i == 0 else VMEM for i in range(len(args))],
        out_specs=jax.tree.map(lambda _: VMEM, outs),
        scratch_shapes=scratch,
        compiler_params=pltpu.CompilerParams(vmem_limit_bytes=vmem << 20),
        cost_estimate=CHEAP,
        name=kernel.__name__,
    )(*args)


def body(sizes, design, local, observed, valid, counts):
    nz, nyl, ncore, nx, nyh = sizes
    z, yl, core, x, yh = (lax.axis_index(name) for name in AXES)
    delta = (z - x) % nx
    rows, width = design.shape
    half, top = width // 2, rows // 2
    down = [(i, (i - 1) % nx) for i in range(nx)]
    up = [(i, (i + 1) % nx) for i in range(nx)]
    swap = [(0, 1), (1, 0)]
    turn = lambda k: [(i, (i + k) % nz) for i in range(nz)]
    high_x = (x >= nx // 2).astype(jnp.int32)
    same = (yl == yh).astype(jnp.int32)
    right = core ^ jnp.where(delta == 2, high_x, yh)
    where = jnp.stack([core, delta, yh, high_x, same, right]).astype(jnp.int32)

    upper, lower = design[:top], design[top:]
    above = lax.ppermute(upper, "x", down)
    below = lax.ppermute(lower, "x", up)
    flip_top = lax.ppermute(upper, "yh", swap)

    wide, sent = shape((half, width), F32), shape((half, width), BF16)
    full, sideways = shape((rows, width), BF16), shape((width, rows), BF16)

    row, low_rows = shape((1, width), F32), 16
    a_high, a_low, residual = eliminate(local, observed, valid, counts)
    own_rows, own, own_keep, own_send, rhs = call(
        own_kernel,
        (full, sideways, wide, shape((half + low_rows, width), BF16), row),
        where, a_high, a_low, residual, design,
        vmem=24,
    )
    del own_rows
    own_got = lax.ppermute(own_send, "core", swap)

    above, below, flip_top, own, lower, own_got = lax.optimization_barrier(
        (above, below, flip_top, own, lower, own_got)
    )
    flip_bottom = lax.ppermute(lower, "yh", swap)
    above2 = lax.ppermute(above, "x", down)
    below2 = lax.ppermute(below, "x", up)

    top_full, top_sideways = shape((top, width), BF16), shape((width, top), BF16)
    near_top, near_bottom, keep, send = call(
        near_kernel,
        (top_full, top_full, shape((2, half, width), F32), shape((2, half, width), BF16)),
        where, a_high, a_low, own, above, below,
        vmem=24,
    )
    got = lax.ppermute(send, "core", swap)
    mine, *ups, rhs = call(
        near_spread_kernel, (wide, sent, sent, sent, row), where, own_keep, keep, rhs, own_got, got,
        scratch=(pltpu.VMEM((nz, half, width), F32),),
    )
    flip_top, near_top, rhs = lax.optimization_barrier((flip_top, near_top, rhs))
    early_turn = lambda k: [
        (a * nx + b, (a + k) % nz * nx + b) for a in range(nz) for b in range(nx) if (a + k - b) % nx != 2
    ]
    ups = [lax.ppermute(v, ("z", "x"), early_turn(k)) for k, v in enumerate(ups, 1)]
    flip_top, flip_top_turned, up_keep, up_send = call(
        middle_kernel, (top_full, top_sideways, wide, sent), where, a_high, a_low, near_top, flip_top,
        vmem=16,
    )

    flip_bottom, above2, below2, flip_top, ups = lax.optimization_barrier(
        (flip_bottom, above2, below2, flip_top, ups)
    )
    early, send = call(near_total_kernel, (wide, sent), mine, *ups, scalars=False)
    early_got = lax.ppermute(send, ("yl", "yh"), [(1, 3), (2, 0)])
    chunks = 2
    size = half // chunks
    pieces = (shape((nz, size, width), F32), shape((nz, size, width), BF16))
    keep, send, flip_bottom, flip_bottom_turned, two = call(
        far_kernel,
        pieces + (top_full, top_sideways, full),
        where, a_high, a_low, own, near_bottom, up_keep, up_send, flip_top, flip_top_turned,
        flip_bottom, above2, below2,
        vmem=28,
    )
    keeps, gots = [keep], [lax.ppermute(send, "core", swap)]
    keep, send = call(
        far_rest_kernel, pieces,
        where, own, near_bottom, up_keep, up_send, flip_top, flip_top_turned, flip_bottom, flip_bottom_turned, two,
        vmem=24,
    )
    keep, send, gots[0] = lax.optimization_barrier((keep, send, gots[0]))
    keeps.append(keep)
    gots.append(lax.ppermute(send, "core", swap))

    late = []
    for chunk, (keep, got) in enumerate(zip(keeps, gots)):
        up = shape((size + (low_rows if chunk == 0 else 0), width), BF16)
        mine, *ups = call(far_spread_kernel, (shape((size, width), F32), up, up, up), where, keep, got, rhs)
        late += [mine] + [lax.ppermute(v, "z", turn(k)) for k, v in enumerate(ups, 1)]
    late, early_got = lax.optimization_barrier((late, early_got))
    keep, send, rhs = call(
        far_total_kernel, (wide, shape((half + low_rows, width), BF16), row), where, rhs, *late
    )
    got = lax.ppermute(send, "yl", swap)

    quad = shape((half, half), BF16)
    placed, mirror, mirror_quad, send, rhs = call(
        place_kernel, (wide, sent, quad, quad, row), where, early, early_got, keep, got, rhs
    )
    pairs = [(a * nx + b, b * nx + a) for a in range(nz) for b in range(nx) if (a - b) % 2]
    mirror = lax.ppermute(mirror, ("z", "x"), pairs)
    pairs = [(a * nx + b, b * nx + a) for a in range(nz) for b in range(nx) if (a - b) % nx == 2]
    mirror_quad = lax.ppermute(mirror_quad, ("z", "x"), pairs)
    got = lax.ppermute(send, "core", swap)
    turned, across = call(turn_kernel, (wide, sent), where, placed, got)
    across = lax.ppermute(across, ("yl", "yh"), [(1, 2), (2, 1)])
    out = call(finish_kernel, wide, where, placed, turned, mirror, mirror_quad, across)
    return out, rhs[0]


def solution(mesh):
    sizes = (4, 2, 2, 4, 2)
    grid = Mesh(mesh.devices.reshape(sizes), AXES)
    arc, col = ("z", "yl", "core"), ("x", "yh")

    def run(design, local_design, observed, valid_mask, counts):
        return jax.shard_map(
            functools.partial(body, sizes),
            mesh=grid,
            in_specs=(P(arc, col), P(None, arc), P(arc), P(arc), P(arc)),
            out_specs=(P(arc, col), P(col)),
            check_vma=False,
        )(design, local_design, observed, valid_mask, counts)

    return run
```

```python
import functools

import jax
import jax.numpy as jnp
from jax import lax
from jax.experimental import pallas as pl
from jax.experimental.pallas import tpu as pltpu
from jax.sharding import Mesh, PartitionSpec as P

LOCAL = 16
SLOTS = 192
AXES = ("z", "yl", "core", "x", "yh")
HIGHEST = lax.Precision.HIGHEST
F32 = jnp.float32
BF16 = jnp.bfloat16
VMEM = pl.BlockSpec(memory_space=pltpu.VMEM)
SMEM = pl.BlockSpec(memory_space=pltpu.SMEM)
PARAMS = pltpu.CompilerParams(vmem_limit_bytes=16 << 20)
LONG = pl.CostEstimate(flops=20_000_000_000, transcendentals=0, bytes_accessed=1)
CHEAP = pl.CostEstimate(flops=1, transcendentals=0, bytes_accessed=1)


def shape(dims, dtype):
    return jax.ShapeDtypeStruct(dims, dtype)


def inner(a, b, contract, precision=None):
    return lax.dot_general(a, b, ((contract[:1], contract[1:]), ((), ())), precision=precision, preferred_element_type=F32)


def iota(dims, axis):
    return lax.broadcasted_iota(jnp.int32, dims, axis)


def eliminate_kernel(counts, block, observed, valid, high, low, residual):
    arcs = block.shape[0]
    eye = (iota((LOCAL, LOCAL), 0) == iota((LOCAL, LOCAL), 1)).astype(F32)
    live, masked, grams = [], [], []
    for a in range(arcs):
        inside = (iota((1, SLOTS), 1) < counts[a]).astype(F32)
        live.append(inside * valid[a : a + 1, :].astype(F32))
        masked.append(block[a] * live[a])
        grams.append((inner(masked[a], block[a], (1, 1), HIGHEST) + eye)[None])
    gram = jnp.concatenate(grams, 0)
    rows, cols = iota(gram.shape, 1), iota(gram.shape, 2)
    for p in range(LOCAL):
        column = gram[:, :, p : p + 1]
        pivot = 1.0 / gram[:, p : p + 1, p : p + 1]
        row = gram[:, p : p + 1, :] * pivot
        swept = jnp.where(rows == p, row, gram - column * row)
        edge = jnp.where(rows == p, pivot, -column * pivot)
        gram = jnp.where(cols == p, edge, swept)
    diagonal = iota((SLOTS, SLOTS), 0) == iota((SLOTS, SLOTS), 1)
    for a in range(arcs):
        weights = jnp.dot(gram[a], masked[a], precision=HIGHEST, preferred_element_type=F32)
        fitted = inner(masked[a], weights, (0, 0), HIGHEST)
        elim = jnp.where(diagonal, live[a], 0.0) - fitted
        top = elim.astype(BF16)
        high[a * SLOTS : (a + 1) * SLOTS, :] = top
        low[a * SLOTS : (a + 1) * SLOTS, :] = (elim - top.astype(F32)).astype(BF16)
        y = observed[a : a + 1, :]
        solved = jnp.sum(weights * y, axis=1, keepdims=True)
        residual[a : a + 1, :] = live[a] * (y - jnp.sum(block[a] * solved, axis=0, keepdims=True))


def eliminate(local, observed, valid, counts):
    arcs = counts.shape[0]
    block = local.reshape(LOCAL, arcs, SLOTS).transpose(1, 0, 2)
    return pl.pallas_call(
        eliminate_kernel,
        out_shape=(
            shape((arcs * SLOTS, SLOTS), BF16),
            shape((arcs * SLOTS, SLOTS), BF16),
            shape((arcs, SLOTS), F32),
        ),
        in_specs=[SMEM, VMEM, VMEM, VMEM],
        out_specs=(VMEM, VMEM, VMEM),
        compiler_params=PARAMS,
        cost_estimate=CHEAP,
        name="eliminate",
    )(counts, block, observed.reshape(arcs, SLOTS), valid.reshape(arcs, SLOTS))


def rounded(high, low, rows):
    first = jnp.dot(high, rows, preferred_element_type=F32)
    return (first + jnp.dot(low, rows, preferred_element_type=F32)).astype(BF16)


def project_into(out, high, low, rows, begin, count, source):
    for i in range(count):
        to = slice((begin + i) * SLOTS, (begin + i + 1) * SLOTS)
        at = slice((source + i) * SLOTS, (source + i + 1) * SLOTS)
        out[to, :] = rounded(high[to, :], low[to, :], rows[at, :])


def project_half(out, high, low, rows, first, count):
    for i in range(count):
        at = slice(i * SLOTS, (i + 1) * SLOTS)
        arc = slice((first + i) * SLOTS, (first + i + 1) * SLOTS)
        out[at, :] = rounded(high[arc, :], low[arc, :], rows[at, :])


def split(core, result, keep, send):
    half = result.shape[0] // 2
    keep[...] = jnp.where(core == 0, result[:half], result[half:])
    send[...] = jnp.where(core == 0, result[half:], result[:half]).astype(BF16)


def parts_of(value):
    one = value.astype(BF16).astype(F32)
    two = (value - one).astype(BF16).astype(F32)
    three = value - one - two
    line = iota((16, value.shape[1]), 0)
    stack = jnp.where(line == 0, one, jnp.where(line == 1, two, jnp.where(line == 2, three, 0.0)))
    return stack.astype(BF16)


def whole_of(block):
    parts = block.astype(F32)
    return (parts[0:1] + parts[1:2]) + parts[2:3]


def own_kernel(where, high, low, residual, rows, out, turned, keep, send, rhs):
    arcs, half = residual.shape[0], keep.shape[0]
    project_into(out, high, low, rows, 0, arcs, 0)
    total = jnp.zeros((1, rows.shape[1]), F32)
    for a in range(arcs):
        stack = parts_of(residual[a : a + 1, :])
        part = jnp.dot(stack, out[a * SLOTS : (a + 1) * SLOTS, :], preferred_element_type=F32)
        total = total + jnp.sum(part, axis=0, keepdims=True)
    rhs[...] = total
    send[half:, :] = parts_of(total)
    turned[...] = out[...].T
    result = jnp.dot(turned[...], out[...], preferred_element_type=F32)
    split(where[0], result, keep, send.at[pl.ds(0, half), :])


def near_kernel(where, high, low, own, above, below, near_top, near_bottom, keep, send):
    arcs = high.shape[0] // SLOTS
    top = above.shape[0]
    project_half(near_top, high, low, above, 0, arcs // 2)
    project_half(near_bottom, high, low, below, arcs // 2, arcs // 2)
    for piece, near in enumerate((near_top, near_bottom)):
        result = jnp.dot(own[:, piece * top : (piece + 1) * top], near[...], preferred_element_type=F32)
        split(where[0], result, keep.at[piece], send.at[piece])


def middle_kernel(where, high, low, near, rows, flip, turned, keep, send):
    top = rows.shape[0]
    project_into(flip, high, low, rows, 0, top // SLOTS, 0)
    turned[...] = flip[...].T
    split(where[0], jnp.dot(turned[...], near[...], preferred_element_type=F32), keep, send)


def far_rows(where, chunk, own, near, done, done_send, flips, turned, two, keep, send):
    size, half = keep.shape[1], own.shape[0] // 2
    top = two.shape[0] // 2
    core, cut_flip, cut_two = where[0], where[2], where[3]
    upper, lower = slice(0, top), slice(top, 2 * top)
    rows = slice(chunk * size, (chunk + 1) * size)

    def lines(ref):
        return jnp.concatenate([ref[rows, :], ref[half + chunk * size : half + (chunk + 1) * size, :]], 0)

    def times(a, b):
        return jnp.dot(a, b, preferred_element_type=F32)

    own_lines, flip_top, flip_bottom = lines(own), lines(turned[0]), lines(turned[1])
    keep[1] = done[rows, :]
    send[1] = done_send[rows, :]
    split(core, times(flip_bottom, near[...]), keep.at[3], send.at[3])

    def quadrants(result, cut, slot, columns):
        first = jnp.where(cut == 0, result[:size, :half], result[:size, half:])
        second = jnp.where(cut == 1, result[size:, :half], result[size:, half:])
        keep[slot, :, columns] = jnp.where(core == 0, first, second)
        send[slot, :, columns] = jnp.where(core == 0, second, first).astype(BF16)

    quadrants(
        times(own_lines[:, upper], flips[0][...]) + times(own_lines[:, lower], flips[1][...]),
        cut_flip, 0, slice(0, half),
    )
    keep[0, :, half:] = jnp.zeros((size, half), F32)
    send[0, :, half:] = jnp.zeros((size, half), BF16)
    quadrants(times(own_lines, two[...]), cut_two, 2, slice(0, half))
    quadrants(
        times(flip_top, two[upper, :]) + times(flip_bottom, two[lower, :]),
        cut_two, 2, slice(half, 2 * half),
    )


def far_kernel(
    where, high, low, own, near, done, done_send, flip_top, top_turned, rows, above, below,
    keep, send, flip_bottom, bottom_turned, two,
):
    arcs = high.shape[0] // SLOTS
    project_half(flip_bottom, high, low, rows, arcs // 2, arcs // 2)
    bottom_turned[...] = flip_bottom[...].T
    project_into(two, high, low, above, 0, arcs // 2, 0)
    project_into(two, high, low, below, arcs // 2, arcs // 2, 0)
    flips, turned = (flip_top, flip_bottom), (top_turned, bottom_turned)
    far_rows(where, 0, own, near, done, done_send, flips, turned, two, keep, send)


def far_rest_kernel(
    where, own, near, done, done_send, flip_top, top_turned, flip_bottom, bottom_turned, two, keep, send
):
    flips, turned = (flip_top, flip_bottom), (top_turned, bottom_turned)
    far_rows(where, 1, own, near, done, done_send, flips, turned, two, keep, send)


def tdot(a, b):
    return inner(a, b, (0, 0))


def spread(where, sums, mine, ups):
    delta = where[1]
    mine[...] = sums[delta]
    for k, up in enumerate(ups, 1):
        up[...] = sums[(delta + k) % 4].astype(BF16)


def near_spread_kernel(where, own, keep, rhs, own_got, got, mine, up1, up2, up3, rhs_sum, sums):
    half = own.shape[0]
    sums[0] = own[...] + own_got[:half, :].astype(F32)
    sums[1] = keep[0] + got[0].astype(F32)
    sums[2] = jnp.zeros(sums.shape[1:], F32)
    sums[3] = keep[1] + got[1].astype(F32)
    spread(where, sums, mine, (up1, up2, up3))
    rhs_sum[...] = rhs[...] + whole_of(own_got[half:, :])


def far_spread_kernel(where, keep, got, rhs, mine, up1, up2, up3):
    delta, size = where[1], keep.shape[1]
    mine[...] = keep[delta] + got[delta].astype(F32)
    for k, up in enumerate((up1, up2, up3), 1):
        slot = (delta + k) % 4
        up[:size, :] = (keep[slot] + got[slot].astype(F32)).astype(BF16)
        if up.shape[0] > size:
            up[size:, :] = parts_of(rhs[...])


def near_total_kernel(mine, one, two, three, total, send):
    total[...] = ((mine[...] + one[...].astype(F32)) + two[...].astype(F32)) + three[...].astype(F32)
    send[...] = total[...].astype(BF16)


def far_total_kernel(with_rhs, where, rhs, mine, one, two, three, keep, send, *rhs_sum):
    size, half = keep.shape[0], keep.shape[1] // 2
    opposite, same = where[1] == 2, where[4] == 1
    first, second, third = (up[:size, :].astype(F32) for up in (one, two, three))
    total = ((mine[...] + first) + second) + third
    turned = jnp.concatenate([total[:, half:], total[:, :half]], 1)
    send[:size, :] = jnp.where(jnp.logical_and(opposite, same), turned, total).astype(BF16)
    keep[...] = jnp.where(jnp.logical_and(opposite, jnp.logical_not(same)), turned, total)
    if with_rhs:
        first, second, third = (whole_of(up[size:, :]) for up in (one, two, three))
        total = (rhs[...] + second) + (first + third)
        rhs_sum[0][...] = total
        send[size:, :] = parts_of(total)


def place(where, near, near_got, keep, got, rows, placed, mirror, quads):
    size, half = keep.shape[0], keep.shape[1] // 2
    delta, same, right = where[1], where[4] == 1, where[5] == 1
    late = keep[...] + got[:size, :].astype(F32)
    early = near[rows, :] + near_got[rows, :].astype(F32)
    total = jnp.where(jnp.logical_and(same, delta != 2), early, late)
    quad = jnp.logical_or(delta == 2, jnp.logical_and(delta == 0, jnp.logical_not(same)))
    placed[rows, :half] = jnp.where(jnp.logical_and(quad, right), 0.0, total[:, :half])
    placed[rows, half:] = jnp.where(quad, jnp.where(right, total[:, :half], 0.0), total[:, half:])
    mirror[...] = placed[rows, :].astype(BF16)
    quads[rows, :] = total[:, :half].astype(BF16)


def place_first_kernel(where, near, near_got, keep, got, rhs, placed, mirror, quads, rhs_sum):
    size = keep.shape[0]
    place(where, near, near_got, keep, got, slice(0, size), placed, mirror, quads)
    rhs_sum[...] = rhs[...] + whole_of(got[size:, :])


def place_last_kernel(where, near, near_got, keep, got, placed_first, quads_first, placed, mirror, quads, core_send):
    size, half = keep.shape[0], placed.shape[0]
    first = slice(0, half - size)
    placed[first, :] = placed_first[first, :]
    quads[first, :] = quads_first[first, :]
    place(where, near, near_got, keep, got, slice(half - size, half), placed, mirror, quads)
    core_send[...] = jnp.where(where[0] == 0, placed[:, half:], placed[:, :half]).astype(BF16)


def turn_kernel(where, placed, got, turned, across):
    half = placed.shape[0]
    core, diagonal = where[0], where[1] == 0
    mine = jnp.where(core == 0, placed[:, :half], placed[:, half:])
    other = got[...].astype(F32)
    first = jnp.where(core == 0, mine, other).T
    second = jnp.where(core == 0, other, mine).T
    turned[:, :half] = first
    turned[:, half:] = second
    across[...] = jnp.where(diagonal, placed[...], turned[...]).astype(BF16)


def base_kernel(where, placed, turned, mirror_first, mirror_last, mirror_quad, base):
    half = base.shape[0]
    size = mirror_first.shape[0]
    diagonal, opposite, same = where[1] == 0, where[1] == 2, where[4] == 1
    left = where[5] == 1
    for side, columns in enumerate((slice(0, half), slice(half, 2 * half))):
        for mirror, rows in ((mirror_first, slice(0, size)), (mirror_last, slice(size, half))):
            quad = jnp.where(left == (side == 0), mirror_quad[rows, :].astype(F32), 0.0)
            near = jnp.where(opposite, quad, mirror[:, columns].astype(F32))
            own = jnp.where(diagonal == same, 0.0, turned[rows, columns])
            direct = jnp.where(diagonal, jnp.where(same, placed[rows, columns], 0.0), near)
            base[rows, columns] = direct + own


def finish_kernel(where, base, across, out):
    same = where[4] == 1
    out[...] = base[...] + jnp.where(same, 0.0, across[...].astype(F32))


def call(kernel, outs, *args, scalars=True, scratch=(), vmem=12, statics=(), cost=CHEAP):
    return pl.pallas_call(
        functools.partial(kernel, *statics),
        out_shape=outs,
        in_specs=[SMEM if scalars and i == 0 else VMEM for i in range(len(args))],
        out_specs=jax.tree.map(lambda _: VMEM, outs),
        scratch_shapes=scratch,
        compiler_params=pltpu.CompilerParams(vmem_limit_bytes=vmem << 20),
        cost_estimate=cost,
        name=kernel.__name__,
    )(*args)


def body(sizes, design, local, observed, valid, counts):
    nz, nyl, ncore, nx, nyh = sizes
    z, yl, core, x, yh = (lax.axis_index(name) for name in AXES)
    delta = (z - x) % nx
    rows, width = design.shape
    half, top = width // 2, rows // 2
    down = [(i, (i - 1) % nx) for i in range(nx)]
    up = [(i, (i + 1) % nx) for i in range(nx)]
    swap = [(0, 1), (1, 0)]
    turn = lambda k: [(i, (i + k) % nz) for i in range(nz)]
    high_x = (x >= nx // 2).astype(jnp.int32)
    same = (yl == yh).astype(jnp.int32)
    right = core ^ jnp.where(delta == 2, high_x, yh)
    where = jnp.stack([core, delta, yh, high_x, same, right]).astype(jnp.int32)

    upper, lower = design[:top], design[top:]
    above = lax.ppermute(upper, "x", down)
    below = lax.ppermute(lower, "x", up)
    flip_top = lax.ppermute(upper, "yh", swap)

    wide, sent = shape((half, width), F32), shape((half, width), BF16)
    full, sideways = shape((rows, width), BF16), shape((width, rows), BF16)

    row, low_rows = shape((1, width), F32), 16
    a_high, a_low, residual = eliminate(local, observed, valid, counts)
    own_rows, own, own_keep, own_send, rhs = call(
        own_kernel,
        (full, sideways, wide, shape((half + low_rows, width), BF16), row),
        where, a_high, a_low, residual, design,
        vmem=24,
    )
    del own_rows
    own_got = lax.ppermute(own_send, "core", swap)

    above, below, flip_top, own, lower, own_got = lax.optimization_barrier(
        (above, below, flip_top, own, lower, own_got)
    )
    flip_bottom = lax.ppermute(lower, "yh", swap)
    above2 = lax.ppermute(above, "x", down)
    below2 = lax.ppermute(below, "x", up)

    top_full, top_sideways = shape((top, width), BF16), shape((width, top), BF16)
    near_top, near_bottom, keep, send = call(
        near_kernel,
        (top_full, top_full, shape((2, half, width), F32), shape((2, half, width), BF16)),
        where, a_high, a_low, own, above, below,
        vmem=24,
    )
    got = lax.ppermute(send, "core", swap)
    mine, *ups, rhs = call(
        near_spread_kernel, (wide, sent, sent, sent, row), where, own_keep, keep, rhs, own_got, got,
        scratch=(pltpu.VMEM((nz, half, width), F32),),
    )
    flip_top, near_top, rhs = lax.optimization_barrier((flip_top, near_top, rhs))
    early_turn = lambda k: [
        (a * nx + b, (a + k) % nz * nx + b) for a in range(nz) for b in range(nx) if (a + k - b) % nx != 2
    ]
    ups = [lax.ppermute(v, ("z", "x"), early_turn(k)) for k, v in enumerate(ups, 1)]
    flip_top, flip_top_turned, up_keep, up_send = call(
        middle_kernel, (top_full, top_sideways, wide, sent), where, a_high, a_low, near_top, flip_top,
        vmem=16,
    )

    flip_bottom, above2, below2, flip_top, ups = lax.optimization_barrier(
        (flip_bottom, above2, below2, flip_top, ups)
    )
    early, send = call(near_total_kernel, (wide, sent), mine, *ups, scalars=False)
    early_got = lax.ppermute(send, ("yl", "yh"), [(1, 3), (2, 0)])
    chunks = 2
    size = half // chunks
    pieces = (shape((nz, size, width), F32), shape((nz, size, width), BF16))
    keep, send, flip_bottom, flip_bottom_turned, two = call(
        far_kernel,
        pieces + (top_full, top_sideways, full),
        where, a_high, a_low, own, near_bottom, up_keep, up_send, flip_top, flip_top_turned,
        flip_bottom, above2, below2,
        vmem=28,
    )
    keeps, gots = [keep], [lax.ppermute(send, "core", swap)]
    keep, send = call(
        far_rest_kernel, pieces,
        where, own, near_bottom, up_keep, up_send, flip_top, flip_top_turned, flip_bottom, flip_bottom_turned, two,
        vmem=24,
    )
    keep, send, gots[0] = lax.optimization_barrier((keep, send, gots[0]))
    keeps.append(keep)
    gots.append(lax.ppermute(send, "core", swap))

    part = shape((size, width), F32)
    sums = []
    for chunk, (keep, got) in enumerate(zip(keeps, gots)):
        up = shape((size + (low_rows if chunk == 0 else 0), width), BF16)
        mine, *ups = call(far_spread_kernel, (part, up, up, up), where, keep, got, rhs)
        sums.append((mine, [lax.ppermute(v, "z", turn(k)) for k, v in enumerate(ups, 1)]))
    halves = []
    for chunk, (mine, ups) in enumerate(sums):
        extra = (row,) if chunk == 0 else ()
        up = shape((size + (low_rows if chunk == 0 else 0), width), BF16)
        keep, send, *rest = call(
            far_total_kernel, (part, up) + extra, where, rhs, mine, *ups, statics=(chunk == 0,)
        )
        if rest:
            (rhs_sum,) = rest
        halves.append((keep, lax.ppermute(send, "yl", swap)))

    beside = [(a * nx + b, b * nx + a) for a in range(nz) for b in range(nx) if (a - b) % 2]
    opposite = [(a * nx + b, b * nx + a) for a in range(nz) for b in range(nx) if (a - b) % nx == 2]
    quad, mirror = shape((half, half), BF16), shape((size, width), BF16)
    placed, mirror_first, quads, rhs = call(
        place_first_kernel, (wide, mirror, quad, row), where, early, early_got, *halves[0], rhs_sum
    )
    mirror_first = lax.ppermute(mirror_first, ("z", "x"), beside)
    placed, mirror_last, quads, send = call(
        place_last_kernel, (wide, mirror, quad, quad), where, early, early_got, *halves[1], placed, quads
    )
    mirror_last = lax.ppermute(mirror_last, ("z", "x"), beside)
    mirror_quad = lax.ppermute(quads, ("z", "x"), opposite)
    got = lax.ppermute(send, "core", swap)
    got, mirror_first = lax.optimization_barrier((got, mirror_first))
    turned, across = call(turn_kernel, (wide, sent), where, placed, got)
    across = lax.ppermute(across, ("yl", "yh"), [(1, 2), (2, 1)])
    base = call(base_kernel, wide, where, placed, turned, mirror_first, mirror_last, mirror_quad, cost=LONG)
    out = call(finish_kernel, wide, where, base, across)
    return out, rhs[0]


def solution(mesh):
    sizes = (4, 2, 2, 4, 2)
    grid = Mesh(mesh.devices.reshape(sizes), AXES)
    arc, col = ("z", "yl", "core"), ("x", "yh")

    def run(design, local_design, observed, valid_mask, counts):
        return jax.shard_map(
            functools.partial(body, sizes),
            mesh=grid,
            in_specs=(P(arc, col), P(None, arc), P(arc), P(arc), P(arc)),
            out_specs=(P(arc, col), P(col)),
            check_vma=False,
        )(design, local_design, observed, valid_mask, counts)

    return run
```

```python
import functools

import jax
import jax.numpy as jnp
from jax import lax
from jax.experimental import pallas as pl
from jax.experimental.pallas import tpu as pltpu
from jax.sharding import Mesh, PartitionSpec as P

LOCAL = 16
SLOTS = 192
AXES = ("z", "yl", "core", "x", "yh")
HIGHEST = lax.Precision.HIGHEST
F32 = jnp.float32
BF16 = jnp.bfloat16
VMEM = pl.BlockSpec(memory_space=pltpu.VMEM)
SMEM = pl.BlockSpec(memory_space=pltpu.SMEM)
PARAMS = pltpu.CompilerParams(vmem_limit_bytes=16 << 20)
LONG = pl.CostEstimate(flops=20_000_000_000, transcendentals=0, bytes_accessed=1)
CHEAP = pl.CostEstimate(flops=1, transcendentals=0, bytes_accessed=1)


def shape(dims, dtype):
    return jax.ShapeDtypeStruct(dims, dtype)


def inner(a, b, contract, precision=None):
    return lax.dot_general(a, b, ((contract[:1], contract[1:]), ((), ())), precision=precision, preferred_element_type=F32)


def iota(dims, axis):
    return lax.broadcasted_iota(jnp.int32, dims, axis)


def eliminate_kernel(counts, block, observed, valid, high, low, residual):
    arcs = block.shape[0]
    eye = (iota((LOCAL, LOCAL), 0) == iota((LOCAL, LOCAL), 1)).astype(F32)
    live, masked, grams = [], [], []
    for a in range(arcs):
        inside = (iota((1, SLOTS), 1) < counts[a]).astype(F32)
        live.append(inside * valid[a : a + 1, :].astype(F32))
        masked.append(block[a] * live[a])
        grams.append((inner(masked[a], block[a], (1, 1), HIGHEST) + eye)[None])
    gram = jnp.concatenate(grams, 0)
    rows, cols = iota(gram.shape, 1), iota(gram.shape, 2)
    for p in range(LOCAL):
        column = gram[:, :, p : p + 1]
        pivot = 1.0 / gram[:, p : p + 1, p : p + 1]
        row = gram[:, p : p + 1, :] * pivot
        swept = jnp.where(rows == p, row, gram - column * row)
        edge = jnp.where(rows == p, pivot, -column * pivot)
        gram = jnp.where(cols == p, edge, swept)
    diagonal = iota((SLOTS, SLOTS), 0) == iota((SLOTS, SLOTS), 1)
    for a in range(arcs):
        weights = jnp.dot(gram[a], masked[a], precision=HIGHEST, preferred_element_type=F32)
        fitted = inner(masked[a], weights, (0, 0), HIGHEST)
        elim = jnp.where(diagonal, live[a], 0.0) - fitted
        top = elim.astype(BF16)
        high[a * SLOTS : (a + 1) * SLOTS, :] = top
        low[a * SLOTS : (a + 1) * SLOTS, :] = (elim - top.astype(F32)).astype(BF16)
        y = observed[a : a + 1, :]
        solved = jnp.sum(weights * y, axis=1, keepdims=True)
        residual[a : a + 1, :] = live[a] * (y - jnp.sum(block[a] * solved, axis=0, keepdims=True))


def eliminate(local, observed, valid, counts):
    arcs = counts.shape[0]
    block = local.reshape(LOCAL, arcs, SLOTS).transpose(1, 0, 2)
    return pl.pallas_call(
        eliminate_kernel,
        out_shape=(
            shape((arcs * SLOTS, SLOTS), BF16),
            shape((arcs * SLOTS, SLOTS), BF16),
            shape((arcs, SLOTS), F32),
        ),
        in_specs=[SMEM, VMEM, VMEM, VMEM],
        out_specs=(VMEM, VMEM, VMEM),
        compiler_params=PARAMS,
        cost_estimate=CHEAP,
        name="eliminate",
    )(counts, block, observed.reshape(arcs, SLOTS), valid.reshape(arcs, SLOTS))


def rounded(high, low, rows):
    first = jnp.dot(high, rows, preferred_element_type=F32)
    return (first + jnp.dot(low, rows, preferred_element_type=F32)).astype(BF16)


def project_into(out, high, low, rows, begin, count, source):
    for i in range(count):
        to = slice((begin + i) * SLOTS, (begin + i + 1) * SLOTS)
        at = slice((source + i) * SLOTS, (source + i + 1) * SLOTS)
        out[to, :] = rounded(high[to, :], low[to, :], rows[at, :])


def project_half(out, high, low, rows, first, count):
    for i in range(count):
        at = slice(i * SLOTS, (i + 1) * SLOTS)
        arc = slice((first + i) * SLOTS, (first + i + 1) * SLOTS)
        out[at, :] = rounded(high[arc, :], low[arc, :], rows[at, :])


def split(core, result, keep, send):
    half = result.shape[0] // 2
    keep[...] = jnp.where(core == 0, result[:half], result[half:])
    send[...] = jnp.where(core == 0, result[half:], result[:half]).astype(BF16)


def parts_of(value):
    one = value.astype(BF16).astype(F32)
    two = (value - one).astype(BF16).astype(F32)
    three = value - one - two
    line = iota((16, value.shape[1]), 0)
    stack = jnp.where(line == 0, one, jnp.where(line == 1, two, jnp.where(line == 2, three, 0.0)))
    return stack.astype(BF16)


def whole_of(block):
    parts = block.astype(F32)
    return (parts[0:1] + parts[1:2]) + parts[2:3]


def own_kernel(where, high, low, residual, rows, out, turned, keep, send, rhs):
    arcs, half = residual.shape[0], keep.shape[0]
    project_into(out, high, low, rows, 0, arcs, 0)
    total = jnp.zeros((1, rows.shape[1]), F32)
    for a in range(arcs):
        stack = parts_of(residual[a : a + 1, :])
        part = jnp.dot(stack, out[a * SLOTS : (a + 1) * SLOTS, :], preferred_element_type=F32)
        total = total + jnp.sum(part, axis=0, keepdims=True)
    rhs[...] = total
    send[half:, :] = parts_of(total)
    turned[...] = out[...].T
    result = jnp.dot(turned[...], out[...], preferred_element_type=F32)
    split(where[0], result, keep, send.at[pl.ds(0, half), :])


def near_kernel(where, high, low, own, above, below, near_top, near_bottom, keep, send):
    arcs = high.shape[0] // SLOTS
    top = above.shape[0]
    project_half(near_top, high, low, above, 0, arcs // 2)
    project_half(near_bottom, high, low, below, arcs // 2, arcs // 2)
    for piece, near in enumerate((near_top, near_bottom)):
        result = jnp.dot(own[:, piece * top : (piece + 1) * top], near[...], preferred_element_type=F32)
        split(where[0], result, keep.at[piece], send.at[piece])


def middle_kernel(where, high, low, near, rows, flip, turned, keep, send):
    top = rows.shape[0]
    project_into(flip, high, low, rows, 0, top // SLOTS, 0)
    turned[...] = flip[...].T
    split(where[0], jnp.dot(turned[...], near[...], preferred_element_type=F32), keep, send)


def far_rows(where, chunk, own, near, done, done_send, flips, turned, two, keep, send):
    size, half = keep.shape[1], own.shape[0] // 2
    top = two.shape[0] // 2
    core, cut_flip, cut_two = where[0], where[2], where[3]
    upper, lower = slice(0, top), slice(top, 2 * top)
    rows = slice(chunk * size, (chunk + 1) * size)

    def lines(ref):
        return jnp.concatenate([ref[rows, :], ref[half + chunk * size : half + (chunk + 1) * size, :]], 0)

    def times(a, b):
        return jnp.dot(a, b, preferred_element_type=F32)

    own_lines, flip_top, flip_bottom = lines(own), lines(turned[0]), lines(turned[1])
    keep[1] = done[rows, :]
    send[1] = done_send[rows, :]
    split(core, times(flip_bottom, near[...]), keep.at[3], send.at[3])

    def quadrants(result, cut, slot, columns):
        first = jnp.where(cut == 0, result[:size, :half], result[:size, half:])
        second = jnp.where(cut == 1, result[size:, :half], result[size:, half:])
        keep[slot, :, columns] = jnp.where(core == 0, first, second)
        send[slot, :, columns] = jnp.where(core == 0, second, first).astype(BF16)

    quadrants(
        times(own_lines[:, upper], flips[0][...]) + times(own_lines[:, lower], flips[1][...]),
        cut_flip, 0, slice(0, half),
    )
    keep[0, :, half:] = jnp.zeros((size, half), F32)
    send[0, :, half:] = jnp.zeros((size, half), BF16)
    quadrants(times(own_lines, two[...]), cut_two, 2, slice(0, half))
    quadrants(
        times(flip_top, two[upper, :]) + times(flip_bottom, two[lower, :]),
        cut_two, 2, slice(half, 2 * half),
    )


def far_kernel(
    where, high, low, own, near, done, done_send, flip_top, top_turned, rows, above, below,
    keep, send, flip_bottom, bottom_turned, two,
):
    arcs = high.shape[0] // SLOTS
    project_half(flip_bottom, high, low, rows, arcs // 2, arcs // 2)
    bottom_turned[...] = flip_bottom[...].T
    project_into(two, high, low, above, 0, arcs // 2, 0)
    project_into(two, high, low, below, arcs // 2, arcs // 2, 0)
    flips, turned = (flip_top, flip_bottom), (top_turned, bottom_turned)
    far_rows(where, 0, own, near, done, done_send, flips, turned, two, keep, send)


def far_rest_kernel(
    where, own, near, done, done_send, flip_top, top_turned, flip_bottom, bottom_turned, two, keep, send
):
    flips, turned = (flip_top, flip_bottom), (top_turned, bottom_turned)
    far_rows(where, 1, own, near, done, done_send, flips, turned, two, keep, send)


def tdot(a, b):
    return inner(a, b, (0, 0))


def spread(where, sums, mine, ups):
    delta = where[1]
    mine[...] = sums[delta]
    for k, up in enumerate(ups, 1):
        up[...] = sums[(delta + k) % 4].astype(BF16)


def near_spread_kernel(where, own, keep, rhs, own_got, got, mine, up1, up2, up3, rhs_sum, sums):
    half = own.shape[0]
    sums[0] = own[...] + own_got[:half, :].astype(F32)
    sums[1] = keep[0] + got[0].astype(F32)
    sums[2] = jnp.zeros(sums.shape[1:], F32)
    sums[3] = keep[1] + got[1].astype(F32)
    spread(where, sums, mine, (up1, up2, up3))
    rhs_sum[...] = rhs[...] + whole_of(own_got[half:, :])


def far_spread_kernel(where, keep, got, rhs, mine, up1, up2, up3):
    delta, size = where[1], keep.shape[1]
    mine[...] = keep[delta] + got[delta].astype(F32)
    for k, up in enumerate((up1, up2, up3), 1):
        slot = (delta + k) % 4
        up[:size, :] = (keep[slot] + got[slot].astype(F32)).astype(BF16)
        if up.shape[0] > size:
            up[size:, :] = parts_of(rhs[...])


def near_total_kernel(mine, one, two, three, total, send):
    total[...] = ((mine[...] + one[...].astype(F32)) + two[...].astype(F32)) + three[...].astype(F32)
    send[...] = total[...].astype(BF16)


def far_total_kernel(with_rhs, where, rhs, mine, one, two, three, keep, send, *rhs_sum):
    size, half = keep.shape[0], keep.shape[1] // 2
    opposite, same = where[1] == 2, where[4] == 1
    first, second, third = (up[:size, :].astype(F32) for up in (one, two, three))
    total = ((mine[...] + first) + second) + third
    turned = jnp.concatenate([total[:, half:], total[:, :half]], 1)
    send[:size, :] = jnp.where(jnp.logical_and(opposite, same), turned, total).astype(BF16)
    keep[...] = jnp.where(jnp.logical_and(opposite, jnp.logical_not(same)), turned, total)
    if with_rhs:
        first, second, third = (whole_of(up[size:, :]) for up in (one, two, three))
        total = (rhs[...] + second) + (first + third)
        rhs_sum[0][...] = total
        send[size:, :] = parts_of(total)


def place(where, near, near_got, keep, got, rows, placed, mirror, quads):
    size, half = keep.shape[0], keep.shape[1] // 2
    delta, same, right = where[1], where[4] == 1, where[5] == 1
    late = keep[...] + got[:size, :].astype(F32)
    early = near[rows, :] + near_got[rows, :].astype(F32)
    total = jnp.where(jnp.logical_and(same, delta != 2), early, late)
    quad = jnp.logical_or(delta == 2, jnp.logical_and(delta == 0, jnp.logical_not(same)))
    placed[rows, :half] = jnp.where(jnp.logical_and(quad, right), 0.0, total[:, :half])
    placed[rows, half:] = jnp.where(quad, jnp.where(right, total[:, :half], 0.0), total[:, half:])
    mirror[...] = placed[rows, :].astype(BF16)
    quads[rows, :] = total[:, :half].astype(BF16)


def place_first_kernel(where, near, near_got, keep, got, rhs, placed, mirror, quads, rhs_sum):
    size = keep.shape[0]
    place(where, near, near_got, keep, got, slice(0, size), placed, mirror, quads)
    rhs_sum[...] = rhs[...] + whole_of(got[size:, :])


def place_last_kernel(where, near, near_got, keep, got, placed_first, quads_first, placed, mirror, quads, core_send):
    size, half = keep.shape[0], placed.shape[0]
    first = slice(0, half - size)
    placed[first, :] = placed_first[first, :]
    quads[first, :] = quads_first[first, :]
    place(where, near, near_got, keep, got, slice(half - size, half), placed, mirror, quads)
    core_send[...] = jnp.where(where[0] == 0, placed[:, half:], placed[:, :half]).astype(BF16)


def turn_kernel(where, placed, got, turned, across):
    half = placed.shape[0]
    core, diagonal = where[0], where[1] == 0
    mine = jnp.where(core == 0, placed[:, :half], placed[:, half:])
    other = got[...].astype(F32)
    first = jnp.where(core == 0, mine, other).T
    second = jnp.where(core == 0, other, mine).T
    turned[:, :half] = first
    turned[:, half:] = second
    across[...] = jnp.where(diagonal, placed[...], turned[...]).astype(BF16)


def base_kernel(where, placed, turned, mirror_first, mirror_last, mirror_quad, base):
    half = base.shape[0]
    size = mirror_first.shape[0]
    diagonal, opposite, same = where[1] == 0, where[1] == 2, where[4] == 1
    left = where[5] == 1
    for side, columns in enumerate((slice(0, half), slice(half, 2 * half))):
        for mirror, rows in ((mirror_first, slice(0, size)), (mirror_last, slice(size, half))):
            quad = jnp.where(left == (side == 0), mirror_quad[rows, :].astype(F32), 0.0)
            near = jnp.where(opposite, quad, mirror[:, columns].astype(F32))
            own = jnp.where(diagonal == same, 0.0, turned[rows, columns])
            direct = jnp.where(diagonal, jnp.where(same, placed[rows, columns], 0.0), near)
            base[rows, columns] = direct + own


def finish_kernel(where, base, across, out):
    same = where[4] == 1
    out[...] = base[...] + jnp.where(same, 0.0, across[...].astype(F32))


def call(kernel, outs, *args, scalars=True, scratch=(), vmem=12, statics=(), cost=CHEAP):
    return pl.pallas_call(
        functools.partial(kernel, *statics),
        out_shape=outs,
        in_specs=[SMEM if scalars and i == 0 else VMEM for i in range(len(args))],
        out_specs=jax.tree.map(lambda _: VMEM, outs),
        scratch_shapes=scratch,
        compiler_params=pltpu.CompilerParams(vmem_limit_bytes=vmem << 20),
        cost_estimate=cost,
        name=kernel.__name__,
    )(*args)


def body(sizes, design, local, observed, valid, counts):
    nz, nyl, ncore, nx, nyh = sizes
    z, yl, core, x, yh = (lax.axis_index(name) for name in AXES)
    delta = (z - x) % nx
    rows, width = design.shape
    half, top = width // 2, rows // 2
    down = [(i, (i - 1) % nx) for i in range(nx)]
    up = [(i, (i + 1) % nx) for i in range(nx)]
    swap = [(0, 1), (1, 0)]
    turn = lambda k: [(i, (i + k) % nz) for i in range(nz)]
    high_x = (x >= nx // 2).astype(jnp.int32)
    same = (yl == yh).astype(jnp.int32)
    right = core ^ jnp.where(delta == 2, high_x, yh)
    where = jnp.stack([core, delta, yh, high_x, same, right]).astype(jnp.int32)

    upper, lower = design[:top], design[top:]
    above = lax.ppermute(upper, "x", down)
    below = lax.ppermute(lower, "x", up)
    flip_top = lax.ppermute(upper, "yh", swap)

    wide, sent = shape((half, width), F32), shape((half, width), BF16)
    full, sideways = shape((rows, width), BF16), shape((width, rows), BF16)

    row, low_rows = shape((1, width), F32), 16
    a_high, a_low, residual = eliminate(local, observed, valid, counts)
    own_rows, own, own_keep, own_send, rhs = call(
        own_kernel,
        (full, sideways, wide, shape((half + low_rows, width), BF16), row),
        where, a_high, a_low, residual, design,
        vmem=24,
    )
    del own_rows
    own_got = lax.ppermute(own_send, "core", swap)

    above, below, flip_top, own, lower, own_got = lax.optimization_barrier(
        (above, below, flip_top, own, lower, own_got)
    )
    flip_bottom = lax.ppermute(lower, "yh", swap)
    above2 = lax.ppermute(above, "x", down)
    below2 = lax.ppermute(below, "x", up)

    top_full, top_sideways = shape((top, width), BF16), shape((width, top), BF16)
    near_top, near_bottom, keep, send = call(
        near_kernel,
        (top_full, top_full, shape((2, half, width), F32), shape((2, half, width), BF16)),
        where, a_high, a_low, own, above, below,
        vmem=24,
    )
    got = lax.ppermute(send, "core", swap)
    mine, *ups, rhs = call(
        near_spread_kernel, (wide, sent, sent, sent, row), where, own_keep, keep, rhs, own_got, got,
        scratch=(pltpu.VMEM((nz, half, width), F32),),
    )
    flip_top, near_top, rhs = lax.optimization_barrier((flip_top, near_top, rhs))
    early_turn = lambda k: [
        (a * nx + b, (a + k) % nz * nx + b) for a in range(nz) for b in range(nx) if (a + k - b) % nx != 2
    ]
    ups = [lax.ppermute(v, ("z", "x"), early_turn(k)) for k, v in enumerate(ups, 1)]
    flip_top, flip_top_turned, up_keep, up_send = call(
        middle_kernel, (top_full, top_sideways, wide, sent), where, a_high, a_low, near_top, flip_top,
        vmem=16,
    )

    flip_bottom, above2, below2, flip_top, ups = lax.optimization_barrier(
        (flip_bottom, above2, below2, flip_top, ups)
    )
    early, send = call(near_total_kernel, (wide, sent), mine, *ups, scalars=False)
    early_send = send
    chunks = 2
    size = half // chunks
    pieces = (shape((nz, size, width), F32), shape((nz, size, width), BF16))
    keep, send, flip_bottom, flip_bottom_turned, two = call(
        far_kernel,
        pieces + (top_full, top_sideways, full),
        where, a_high, a_low, own, near_bottom, up_keep, up_send, flip_top, flip_top_turned,
        flip_bottom, above2, below2,
        vmem=28,
    )
    keeps, gots = [keep], [lax.ppermute(send, "core", swap)]
    keep, send = call(
        far_rest_kernel, pieces,
        where, own, near_bottom, up_keep, up_send, flip_top, flip_top_turned, flip_bottom, flip_bottom_turned, two,
        vmem=24,
    )
    keep, send, gots[0] = lax.optimization_barrier((keep, send, gots[0]))
    keeps.append(keep)
    gots.append(lax.ppermute(send, "core", swap))

    part = shape((size, width), F32)
    sums = []
    for chunk, (keep, got) in enumerate(zip(keeps, gots)):
        up = shape((size + (low_rows if chunk == 0 else 0), width), BF16)
        mine, *ups = call(far_spread_kernel, (part, up, up, up), where, keep, got, rhs)
        if chunk:
            ups[0], early_send = lax.optimization_barrier((ups[0], early_send))
        sums.append((mine, [lax.ppermute(v, "z", turn(k)) for k, v in enumerate(ups, 1)]))
    early_got = lax.ppermute(early_send, ("yl", "yh"), [(1, 3), (2, 0)])
    halves = []
    for chunk, (mine, ups) in enumerate(sums):
        extra = (row,) if chunk == 0 else ()
        up = shape((size + (low_rows if chunk == 0 else 0), width), BF16)
        keep, send, *rest = call(
            far_total_kernel, (part, up) + extra, where, rhs, mine, *ups, statics=(chunk == 0,)
        )
        if rest:
            (rhs_sum,) = rest
        halves.append((keep, lax.ppermute(send, "yl", swap)))

    beside = [(a * nx + b, b * nx + a) for a in range(nz) for b in range(nx) if (a - b) % 2]
    opposite = [(a * nx + b, b * nx + a) for a in range(nz) for b in range(nx) if (a - b) % nx == 2]
    quad, mirror = shape((half, half), BF16), shape((size, width), BF16)
    placed, mirror_first, quads, rhs = call(
        place_first_kernel, (wide, mirror, quad, row), where, early, early_got, *halves[0], rhs_sum
    )
    mirror_first = lax.ppermute(mirror_first, ("z", "x"), beside)
    placed, mirror_last, quads, send = call(
        place_last_kernel, (wide, mirror, quad, quad), where, early, early_got, *halves[1], placed, quads
    )
    mirror_last = lax.ppermute(mirror_last, ("z", "x"), beside)
    mirror_quad = lax.ppermute(quads, ("z", "x"), opposite)
    got = lax.ppermute(send, "core", swap)
    got, mirror_first = lax.optimization_barrier((got, mirror_first))
    turned, across = call(turn_kernel, (wide, sent), where, placed, got)
    across = lax.ppermute(across, ("yl", "yh"), [(1, 2), (2, 1)])
    base = call(base_kernel, wide, where, placed, turned, mirror_first, mirror_last, mirror_quad, cost=LONG)
    out = call(finish_kernel, wide, where, base, across)
    return out, rhs[0]


def solution(mesh):
    sizes = (4, 2, 2, 4, 2)
    grid = Mesh(mesh.devices.reshape(sizes), AXES)
    arc, col = ("z", "yl", "core"), ("x", "yh")

    def run(design, local_design, observed, valid_mask, counts):
        return jax.shard_map(
            functools.partial(body, sizes),
            mesh=grid,
            in_specs=(P(arc, col), P(None, arc), P(arc), P(arc), P(arc)),
            out_specs=(P(arc, col), P(col)),
            check_vma=False,
        )(design, local_design, observed, valid_mask, counts)

    return run
```
